32 devices in a mesh: dp: 2 (over y), fsdp: 16 (over z, x, core).
Axes of the slice: x: 2, y: 2, z: 4, core: 2. Of those that a mesh axis runs over, the one named last changes fastest.
Arguments:
- images: bfloat16 [256, 257, 1280], P(('dp', 'fsdp')), may hold values from -6 to 6
- cotangent: bfloat16 [256, 257, 1280], P(('dp', 'fsdp')), may hold values from -6 to 6
- w_qkv: bfloat16 [1280, 3840], P('fsdp')
- w_out: bfloat16 [1280, 1280], P('fsdp'), may hold values from -3 to 3
- w_up: bfloat16 [1280, 5120], P('fsdp'), may hold values from -0.15625 to 0.15625
- w_down: bfloat16 [5120, 1280], P('fsdp'), may hold values from -0.078125 to 0.078125
- b_qv: bfloat16 [2560], P('fsdp'), may hold values from -3 to 3
- b_out: bfloat16 [1280], P('fsdp'), may hold values from -3 to 3
- b_up: bfloat16 [5120], P('fsdp'), may hold values from -3 to 3
- b_down: bfloat16 [1280], P('fsdp'), may hold values from -3 to 3
- first_norm_scale: bfloat16 [1280], P('fsdp'), may hold values from 0.099609375 to 1.8984375
- first_norm_bias: bfloat16 [1280], P('fsdp'), may hold values from -3 to 3
- second_norm_scale: bfloat16 [1280], P('fsdp'), may hold values from 0.099609375 to 1.8984375
- second_norm_bias: bfloat16 [1280], P('fsdp'), may hold values from -3 to 3
Outputs:
- result: float32 [256, 257, 1280], P(('dp', 'fsdp'))
- d_images: float32 [256, 257, 1280], P(('dp', 'fsdp'))
- g_qkv: float32 [1280, 3840], P('fsdp')
- g_out: float32 [1280, 1280], P('fsdp')
- g_up: float32 [1280, 5120], P('fsdp')
- g_down: float32 [5120, 1280], P('fsdp')
- g_b_qv: float32 [2560], P('fsdp')
- g_b_out: float32 [1280], P('fsdp')
- g_b_up: float32 [5120], P('fsdp')
- g_b_down: float32 [1280], P('fsdp')
- g_gain_one: float32 [1280], P('fsdp')
- g_shift_one: float32 [1280], P('fsdp')
- g_gain_two: float32 [1280], P('fsdp')
- g_shift_two: float32 [1280], P('fsdp')
The draws below stay inside these ranges and needn't reach their ends.
All inputs are finite; a program needn't handle non-finite values.
Results may differ from the reference program's by a relative error of at most 0.012.
Values may be sent and summed in bfloat16 or wider, within the bound.
No kernel may reach another device: no remote copies, remote signals or barrier semaphores. Data moves between devices by JAX's collectives and lax.ppermute only.
A program may use at most 512 MiB of HBM per device.

```python
import jax
import jax.numpy as jnp
from jax import lax

D = 1280
H = 16
HD = 80
FF = 5120
SEQ = 257
IMAGES = 256


def draw_w_qkv(key, part):
    first_residual = jax.random.fold_in(jax.random.fold_in(key, 11), 0)
    weights = jnp.clip(jax.random.normal(first_residual, (D, 3 * D), jnp.float32), -5.0, 5.0) * D ** (-0.5)
    return weights.astype(jnp.bfloat16)


def levels(rng, extent, cuts, least, largest):
    factor_of = 1.0
    for position, blocks in cuts:
        draws = jax.random.uniform(jax.random.fold_in(jax.random.fold_in(rng, 6), position), (blocks,), jnp.float32, least / len(cuts), largest / len(cuts))
        factor_of = factor_of * jnp.repeat(jnp.exp(draws), extent[position] // blocks).reshape((-1,) + (1,) * (len(extent) - 1 - position))
    return factor_of


def bell_draw(own_key, dims, spread, most, cuts=(), held_as=jnp.bfloat16):
    values = spread * jax.random.normal(own_key, dims, jnp.float32)
    if cuts:
        values = values * levels(own_key, dims, cuts, -0.22, 0.18)
    return jnp.clip(values, -most, most).astype(held_as)


def setup_inputs(seed: int = 0) -> dict:
    key_list = jax.random.split(jax.random.key(seed), 15)
    images = bell_draw(key_list[0], (IMAGES, SEQ, D), 1.0, 6.0, ((0, 32),))
    cotangent = bell_draw(key_list[1], (IMAGES, SEQ, D), 1.0, 6.0, ((0, 32),))
    w_qkv = draw_w_qkv(jax.random.fold_in(key_list[14], 71), 0)
    w_out = bell_draw(key_list[3], (D, D), (max(D // SEQ, 1)) ** -0.5, 3.0, ((0, 16),))
    w_up = bell_draw(key_list[4], (D, FF), D ** -0.5, 0.15625, ((0, 16),))
    w_down = bell_draw(key_list[5], (FF, D), FF ** -0.5, 0.078125, ((0, 16),))
    b_qv = bell_draw(key_list[6], (2 * D,), 0.5, 3.0, ((0, 16),))
    b_out = bell_draw(key_list[7], (D,), 0.5, 3.0, ((0, 16),))
    b_up = bell_draw(key_list[8], (FF,), 0.5, 3.0, ((0, 16),))
    b_down = bell_draw(key_list[9], (D,), 0.5, 3.0, ((0, 16),))
    first_norm_scale = jnp.clip(1.0 + 0.18 * jax.random.normal(key_list[10], (D,), jnp.float32), 0.099609375, 1.8984375).astype(jnp.bfloat16)
    first_norm_bias = bell_draw(key_list[11], (D,), 0.5, 3.0, ((0, 16),))
    second_norm_scale = jnp.clip(1.0 + 0.18 * jax.random.normal(key_list[12], (D,), jnp.float32), 0.099609375, 1.8984375).astype(jnp.bfloat16)
    second_norm_bias = bell_draw(key_list[13], (D,), 0.5, 3.0, ((0, 16),))
    return dict(images=images, cotangent=cotangent, w_qkv=w_qkv, w_out=w_out, w_up=w_up, w_down=w_down, b_qv=b_qv, b_out=b_out, b_up=b_up, b_down=b_down, first_norm_scale=first_norm_scale, first_norm_bias=first_norm_bias, second_norm_scale=second_norm_scale, second_norm_bias=second_norm_bias)


EPS = 1e-06

def matmul(left, right):
    return jnp.dot(left, right, preferred_element_type=jnp.float32)

def batched(form, left, right):
    return jnp.einsum(form, left.astype(jnp.float32), right.astype(jnp.float32))

def layer_norm_forward(token_rows, norm_scale, norm_bias):
    centered_rows = token_rows - lax.optimization_barrier(jnp.mean(token_rows, -1, keepdims=True))
    inverse_deviation = lax.rsqrt(lax.optimization_barrier(jnp.mean(centered_rows * centered_rows, -1, keepdims=True)) + EPS)
    standardized_rows = centered_rows * inverse_deviation
    normalized_rows = (standardized_rows * norm_scale.astype(jnp.float32) + norm_bias.astype(jnp.float32)).astype(jnp.bfloat16)
    return (standardized_rows, inverse_deviation, normalized_rows)

def layer_norm_backward(incoming_gradient, standardized_rows, inverse_deviation, norm_scale):
    scaled_rows = incoming_gradient * norm_scale.astype(jnp.float32)
    first_residual = lax.optimization_barrier(jnp.mean(scaled_rows, -1, keepdims=True))
    second_residual = lax.optimization_barrier(jnp.mean(scaled_rows * standardized_rows, -1, keepdims=True))
    input_gradient = inverse_deviation * (scaled_rows - first_residual - standardized_rows * second_residual)
    return (input_gradient, lax.optimization_barrier(jnp.sum(incoming_gradient * standardized_rows, 0)), lax.optimization_barrier(jnp.sum(incoming_gradient, 0)))

def split_heads(packed_projection, count, length):
    query = packed_projection[:, :D].reshape(count, length, H, HD)
    keys_all = packed_projection[:, D:2 * D].reshape(count, length, H, HD)
    values = packed_projection[:, 2 * D:].reshape(count, length, H, HD)
    return (query, keys_all, values)

def forward(block, params):
    w_qkv, w_out, w_up, w_down, b_qv, b_out, b_up, b_down, first_norm_scale, first_norm_bias, second_norm_scale, second_norm_bias = params
    count, length, width = block.shape
    token_rows = block.reshape(count * length, width).astype(jnp.float32)
    first_standardized, first_inverse_deviation, first_normalized = layer_norm_forward(token_rows, first_norm_scale, first_norm_bias)
    bias_all = jnp.concatenate([b_qv[:D].astype(jnp.float32), jnp.zeros((D,), jnp.float32), b_qv[D:].astype(jnp.float32)])
    packed_projection = (matmul(first_normalized, w_qkv) + bias_all).astype(jnp.bfloat16)
    query, keys_all, values = split_heads(packed_projection, count, length)
    scores = batched('bqhd,bkhd->bhqk', query, keys_all) * HD ** (-0.5)
    top = lax.optimization_barrier(jnp.max(scores, -1, keepdims=True))
    log_exponent_sum = top + jnp.log(lax.optimization_barrier(jnp.sum(jnp.exp(scores - top), -1, keepdims=True)))
    probs = jnp.exp(scores - log_exponent_sum).astype(jnp.bfloat16)
    attention_mixture = batched('bhqk,bkhd->bqhd', probs, values).astype(jnp.bfloat16).reshape(count * length, width)
    hidden_state = token_rows + matmul(attention_mixture, w_out) + b_out.astype(jnp.float32)
    second_standardized, second_inverse_deviation, second_normalized = layer_norm_forward(hidden_state, second_norm_scale, second_norm_bias)
    inner_activation = matmul(second_normalized, w_up) + b_up.astype(jnp.float32)
    activation_input = jax.nn.gelu(inner_activation, approximate=False).astype(jnp.bfloat16)
    result = hidden_state + matmul(activation_input, w_down) + b_down.astype(jnp.float32)
    saved_residuals = (first_standardized, first_inverse_deviation, first_normalized, packed_projection, log_exponent_sum, attention_mixture, second_standardized, second_inverse_deviation, second_normalized, inner_activation, activation_input)
    return (result.reshape(count, length, width), saved_residuals)

def backward(cotangent, saved_residuals, params):
    w_qkv, w_out, w_up, w_down, b_qv, b_out, b_up, b_down, first_norm_scale, first_norm_bias, second_norm_scale, second_norm_bias = params
    first_standardized, first_inverse_deviation, first_normalized, packed_projection, log_exponent_sum, attention_mixture, second_standardized, second_inverse_deviation, second_normalized, inner_activation, activation_input = saved_residuals
    count, length, width = cotangent.shape
    grad_rows = cotangent.reshape(count * length, width)
    grad_wide = grad_rows.astype(jnp.float32)
    g_down = matmul(activation_input.T, grad_rows)
    gb_down = lax.optimization_barrier(jnp.sum(grad_wide, 0))
    d_active = matmul(grad_rows, w_down.T)
    slope = 0.5 * (1.0 + jax.scipy.special.erf(inner_activation * 0.7071067811865476)) + inner_activation * jnp.exp(-0.5 * inner_activation * inner_activation) * 0.3989422804014327
    d_inner = d_active * slope
    gb_up = lax.optimization_barrier(jnp.sum(d_inner, 0))
    d_inner_b = d_inner.astype(jnp.bfloat16)
    g_up = matmul(second_normalized.T, d_inner_b)
    second_normalized_gradient = matmul(d_inner_b, w_up.T)
    hidden_norm_gradient, second_scale_gradient, second_bias_gradient = layer_norm_backward(second_normalized_gradient, second_standardized, second_inverse_deviation, second_norm_scale)
    d_hidden = grad_wide + hidden_norm_gradient
    d_hidden_b = d_hidden.astype(jnp.bfloat16)
    g_out = matmul(attention_mixture.T, d_hidden_b)
    gb_out = lax.optimization_barrier(jnp.sum(d_hidden, 0))
    d_mixed = matmul(d_hidden_b, w_out.T).astype(jnp.bfloat16)
    query, keys_all, values = split_heads(packed_projection, count, length)
    d_heads = d_mixed.reshape(count, length, H, HD)
    mixed_heads = attention_mixture.reshape(count, length, H, HD)
    scores = batched('bqhd,bkhd->bhqk', query, keys_all) * HD ** (-0.5)
    probs_wide = jnp.exp(scores - log_exponent_sum)
    probs = probs_wide.astype(jnp.bfloat16)
    d_values = batched('bhqk,bqhd->bkhd', probs, d_heads)
    d_probs = batched('bqhd,bkhd->bhqk', d_heads, values)
    delta = lax.optimization_barrier(jnp.sum(d_heads.astype(jnp.float32) * mixed_heads.astype(jnp.float32), -1))
    delta = jnp.transpose(delta, (0, 2, 1))[..., None]
    d_scores = (probs_wide * (d_probs - delta) * HD ** (-0.5)).astype(jnp.bfloat16)
    d_query = batched('bhqk,bkhd->bqhd', d_scores, keys_all).reshape(count * length, width)
    d_keys = batched('bhqk,bqhd->bkhd', d_scores, query).reshape(count * length, width)
    d_values = d_values.reshape(count * length, width)
    gb_qv = jnp.concatenate([lax.optimization_barrier(jnp.sum(d_query, 0)), lax.optimization_barrier(jnp.sum(d_values, 0))])
    d_packed = jnp.concatenate([d_query, d_keys, d_values], 1).astype(jnp.bfloat16)
    g_qkv = matmul(first_normalized.T, d_packed)
    first_normalized_gradient = matmul(d_packed, w_qkv.T)
    row_norm_gradient, first_scale_gradient, first_bias_gradient = layer_norm_backward(first_normalized_gradient, first_standardized, first_inverse_deviation, first_norm_scale)
    d_rows = d_hidden + row_norm_gradient
    grads = (g_qkv, g_out, g_up, g_down, gb_qv, gb_out, gb_up, gb_down, first_scale_gradient, first_bias_gradient, second_scale_gradient, second_bias_gradient)
    return (d_rows.reshape(count, length, width), grads)

def reference(images, cotangent, w_qkv, w_out, w_up, w_down, b_qv, b_out, b_up, b_down, first_norm_scale, first_norm_bias, second_norm_scale, second_norm_bias):
    params = (w_qkv, w_out, w_up, w_down, b_qv, b_out, b_up, b_down, first_norm_scale, first_norm_bias, second_norm_scale, second_norm_bias)
    blocks = images.reshape(IMAGES // 16, 16, SEQ, D)
    cot_blocks = cotangent.reshape(IMAGES // 16, 16, SEQ, D)
    start = tuple((jnp.zeros(p.shape, jnp.float32) for p in params))

    def one_block(carry, pair):
        block, cot = pair
        result, saved_residuals = forward(block, params)
        d_rows, grads = backward(cot, saved_residuals, params)
        return (tuple((c + g for c, g in zip(carry, grads))), (result, d_rows))
    totals, (results, d_images) = lax.scan(one_block, start, (blocks, cot_blocks))
    return (results.reshape(IMAGES, SEQ, D), d_images.reshape(IMAGES, SEQ, D), totals[0], totals[1], totals[2], totals[3], totals[4], totals[5], totals[6], totals[7], totals[8], totals[9], totals[10], totals[11])
```

```python
import math

import jax
import jax.numpy as jnp
from jax import lax
from jax.experimental import pallas as pl
from jax.experimental.pallas import tpu as pltpu
from jax.sharding import Mesh
from jax.sharding import PartitionSpec as P

D = 1280
H = 16
HD = 80
FF = 5120
SEQ = 257
SP = 264
GROUP = 8
GW = GROUP * HD
EPS = 1e-06
SCALE = HD ** (-0.5)
NT = (((1,), (1,)), ((), ()))
BF = jnp.bfloat16
F32 = jnp.float32


def dot_nt(left, right):
    return lax.dot_general(left, right, NT, preferred_element_type=F32)


def dot_nn(left, right):
    return jnp.dot(left, right, preferred_element_type=F32)


def pad_rows(rows):
    return jnp.concatenate([rows, jnp.zeros((SP - SEQ, rows.shape[1]), rows.dtype)], 0)


def fold_rows(rows):
    return jnp.sum(rows.reshape(rows.shape[0] // 8, 8, rows.shape[1]), 0)


def standardize(rows):
    centered = rows - jnp.mean(rows, -1, keepdims=True)
    inverse = lax.rsqrt(jnp.mean(centered * centered, -1, keepdims=True) + EPS)
    return centered * inverse, inverse


def norm_gradient(e, xhat, inverse, gain):
    scaled = e * gain
    first = jnp.mean(scaled, -1, keepdims=True)
    second = jnp.mean(scaled * xhat, -1, keepdims=True)
    return inverse * (scaled - first - xhat * second)


def cost(flops, arrays):
    moved = sum(math.prod(a.shape) * a.dtype.itemsize for a in arrays)
    return pl.CostEstimate(flops=int(flops), transcendentals=0, bytes_accessed=moved)


def call(kernel, n, ins, outs, name, flops=0, scratch=(), first=0, alias=None):
    def spec(shape, kind):
        if kind == "raw":
            return pl.BlockSpec(memory_space=pl.ANY)
        if kind == "scalars":
            return pl.BlockSpec(memory_space=pltpu.SMEM)
        if kind == "image":
            return pl.BlockSpec((1,) + tuple(shape[1:]), lambda i: (i + first,) + (0,) * (len(shape) - 1))
        if kind == "whole":
            return pl.BlockSpec(tuple(shape), lambda i: (0,) * len(shape), pipeline_mode=pl.Buffered(1))
        return pl.BlockSpec(tuple(shape), lambda i: (0,) * len(shape))

    return pl.pallas_call(
        kernel,
        grid=(n,),
        in_specs=[spec(a.shape, k) for a, k in ins],
        out_specs=[spec(a.shape, k) for a, k in outs],
        out_shape=[a for a, _ in outs],
        scratch_shapes=list(scratch),
        input_output_aliases=alias or {},
        compiler_params=pltpu.CompilerParams(vmem_limit_bytes=60 << 20),
        cost_estimate=cost(flops, [a for a, _ in ins] + [a for a, _ in outs]),
        name=name,
    )(*[a for a, _ in ins])


def accumulate(ref, value):
    @pl.when(pl.program_id(0) == 0)
    def _():
        ref[...] = jnp.zeros_like(ref)
    ref[...] += value


def prepare_kernel(x_ref, c_ref, gain_ref, shift_ref, normed_ref, cpad_ref, sum_ref):
    xhat, _ = standardize(x_ref[0].astype(F32))
    normed = xhat * gain_ref[...] + shift_ref[...]
    normed_ref[0] = pad_rows(normed).astype(BF)
    c = pad_rows(c_ref[0].astype(F32))
    cpad_ref[0] = c.astype(BF)
    accumulate(sum_ref, fold_rows(c))


def qkv_kernel(w_ref, normed_ref, bias_ref, packed_ref):
    for j in range(packed_ref.shape[2] // D):
        cols = slice(j * D, (j + 1) * D)
        packed_ref[0, :, cols] = (dot_nn(normed_ref[0], w_ref[:, cols]) + bias_ref[:, cols]).astype(BF)


def drop_tail(rows):
    tail = rows[SP - 8:]
    keep = lax.broadcasted_iota(jnp.int32, tail.shape, 0) < SEQ - (SP - 8)
    return jnp.concatenate([rows[:SP - 8], jnp.where(keep, tail, 0.0)], 0)


def attention_kernel(packed_ref, mixed_ref, lse_ref):
    def group(g, carry):
        base = g * GW
        here = pl.ds(pl.multiple_of(base, 128), GW)
        queries, keys, values = [
            packed_ref[0, :, pl.ds(pl.multiple_of(part * D + base, 128), GW)] for part in range(3)]
        values_t = values.astype(F32).T.astype(BF)
        outs, lses = [], []
        for j in range(GROUP):
            head = slice(j * HD, (j + 1) * HD)
            s = dot_nt(keys[:, head], queries[:, head])
            tail = s[SP - 8:]
            keep = lax.broadcasted_iota(jnp.int32, tail.shape, 0) < SEQ - (SP - 8)
            s = jnp.concatenate([s[:SP - 8], jnp.where(keep, tail, -1e30)], 0) * SCALE
            top = jnp.max(s, 0, keepdims=True)
            e = jnp.exp(s - top)
            total = jnp.sum(e, 0, keepdims=True)
            o = dot_nn(values_t[head], e.astype(BF)) * (1.0 / total)
            outs.append(o)
            lses.append(top + jnp.log(total))
        mixed_ref[0, :, pl.ds(pl.multiple_of(base, 128), GW)] = jnp.concatenate(outs, 0).T.astype(BF)
        lse_ref[0, pl.ds(pl.multiple_of(g * GROUP, 8), GROUP), :] = jnp.concatenate(lses, 0)
        return carry
    lax.fori_loop(0, H // GROUP, group, 0)


def out_kernel(w_ref, x_ref, mixed_ref, bias_ref, gain_ref, shift_ref, hidden_ref, normed_ref):
    hidden = pad_rows(x_ref[0].astype(F32)) + dot_nn(mixed_ref[0], w_ref[...]) + bias_ref[...]
    hidden_ref[0] = hidden
    xhat, _ = standardize(hidden)
    normed = xhat * gain_ref[...] + shift_ref[...]
    keep = lax.broadcasted_iota(jnp.int32, normed.shape, 0) < SEQ
    normed_ref[0] = jnp.where(keep, normed, 0.0).astype(BF)


CHUNK = 512


def up_kernel(w_ref, normed_ref, bias_ref, active_ref, slope_ref):
    normed = normed_ref[0]

    def step(j, carry):
        cols = pl.ds(pl.multiple_of(j * CHUNK, CHUNK), CHUNK)
        u = dot_nn(normed, w_ref[:, cols]) + bias_ref[:, cols]
        cdf = 0.5 * (1.0 + lax.erf(u * 0.7071067811865476))
        active_ref[0, :, cols] = (u * cdf).astype(BF)
        slope_ref[0, :, cols] = (cdf + u * jnp.exp(-0.5 * u * u) * 0.3989422804014327).astype(BF)
        return carry
    lax.fori_loop(0, FF // CHUNK, step, 0)


def down_kernel(w_ref, active_ref, hidden_ref, bias_ref, result_ref):
    result = hidden_ref[0] + dot_nn(active_ref[0], w_ref[...]) + bias_ref[...]
    result_ref[0] = result[:SEQ]


def down_back_kernel(w_ref, c_ref, slope_ref, dinner_ref, sum_ref):
    c = c_ref[0]

    @pl.when(pl.program_id(0) == 0)
    def _():
        sum_ref[...] = jnp.zeros_like(sum_ref)

    def step(j, carry):
        rows = pl.ds(pl.multiple_of(j * CHUNK, CHUNK), CHUNK)
        d = dot_nt(c, w_ref[rows, :]) * slope_ref[0, :, rows].astype(F32)
        dinner_ref[0, :, rows] = d.astype(BF)
        sum_ref[:, rows] += fold_rows(d)
        return carry
    lax.fori_loop(0, FF // CHUNK, step, 0)


def up_back_kernel(w_up_ref, w_out_ref, dinner_ref, hidden_ref, c_ref, gain_ref,
                   dhidden_ref, dhidden_b_ref, dmixed_ref, sum_gain_ref, sum_shift_ref, sum_out_ref):
    e = dot_nt(dinner_ref[0], w_up_ref[...])
    xhat, inverse = standardize(hidden_ref[0])
    dhidden = c_ref[0].astype(F32) + norm_gradient(e, xhat, inverse, gain_ref[...])
    dhidden_ref[0] = dhidden
    dhidden_b = dhidden.astype(BF)
    dhidden_b_ref[0] = dhidden_b
    dmixed_ref[0] = dot_nt(dhidden_b, w_out_ref[...]).astype(BF)
    accumulate(sum_gain_ref, fold_rows(e * xhat))
    accumulate(sum_shift_ref, fold_rows(e))
    accumulate(sum_out_ref, fold_rows(dhidden))


def attention_back_kernel(packed_ref, mixed_ref, dmixed_ref, lse_ref, dpacked_ref, sum_ref):
    @pl.when(pl.program_id(0) == 0)
    def _():
        sum_ref[...] = jnp.zeros_like(sum_ref)

    def group(g, carry):
        base = g * GW
        here = pl.ds(pl.multiple_of(base, 128), GW)
        queries, keys, values = [
            packed_ref[0, :, pl.ds(pl.multiple_of(part * D + base, 128), GW)] for part in range(3)]
        grads = dmixed_ref[0, :, here]
        product = (grads.astype(F32) * mixed_ref[0, :, here].astype(F32)).T
        keys_t = keys.astype(F32).T.astype(BF)
        lse = lse_ref[0, pl.ds(pl.multiple_of(g * GROUP, 8), GROUP), :]
        dq, dk, dv = [], [], []
        for j in range(GROUP):
            head = slice(j * HD, (j + 1) * HD)
            q, k, v, dm = queries[:, head], keys[:, head], values[:, head], grads[:, head]
            delta = jnp.sum(product[head], 0, keepdims=True)
            p = drop_tail(jnp.exp(dot_nt(k, q) * SCALE - lse[j:j + 1]))
            dv.append(dot_nn(p.astype(BF), dm))
            ds = (p * (dot_nt(v, dm) - delta) * SCALE).astype(BF)
            dk.append(dot_nn(ds, q))
            dq.append(dot_nn(keys_t[head], ds))
        dq = jnp.concatenate(dq, 0).T
        dk = jnp.concatenate(dk, 1)
        dv = jnp.concatenate(dv, 1)
        def out(part):
            return pl.ds(pl.multiple_of(part * D + base, 128), GW)
        keep = lax.broadcasted_iota(jnp.int32, dq.shape, 0) < SEQ
        dq = jnp.where(keep, dq, 0.0)
        dpacked_ref[0, :, out(0)] = dq.astype(BF)
        dpacked_ref[0, :, out(1)] = dk.astype(BF)
        dpacked_ref[0, :, out(2)] = dv.astype(BF)
        sum_ref[:, out(0)] += fold_rows(dq)
        sum_ref[:, out(1)] += fold_rows(dv)
        return carry
    lax.fori_loop(0, H // GROUP, group, 0)


def qkv_back_kernel(w_ref, dpacked_ref, x_ref, dhidden_ref, gain_ref, *refs):
    dimages_ref, sum_gain_ref, sum_shift_ref = refs[-3:]
    e = dot_nt(dpacked_ref[0], w_ref[...])[:SEQ]
    xhat, inverse = standardize(x_ref[0].astype(F32))
    dimages_ref[0] = dhidden_ref[0, :SEQ] + norm_gradient(e, xhat, inverse, gain_ref[...])
    accumulate(sum_gain_ref, fold_rows(pad_rows(e * xhat)))
    accumulate(sum_shift_ref, fold_rows(pad_rows(e)))


def sds(*shape, dtype=BF):
    return jax.ShapeDtypeStruct(shape, dtype)


def weighted(kernel, plans):
    total = sum(len(plan) for plan in plans)

    def run(*refs):
        pieces, rest = refs[:total], refs[total:]
        places, rest = rest[:len(plans)], rest[len(plans):]
        own, scratch = rest[:len(rest) - 2 * len(plans)], rest[len(rest) - 2 * len(plans):]
        weights, sems = scratch[0::2], scratch[1::2]

        @pl.when(pl.program_id(0) == 0)
        def _():
            copies, first = [], 0
            for plan, place, weight, sem in zip(plans, places, weights, sems):
                n = 0
                for count, there, here, width in plan:
                    rows = pieces[first].shape[1]
                    for k in range(count):
                        at = pl.ds(pl.multiple_of(place[0, n] * rows, 16), rows)
                        cols = pl.ds(pl.multiple_of(here + place[1, n] * width, 128), width)
                        copies.append(pltpu.make_async_copy(
                            pieces[first].at[k, :, there:there + width], weight.at[at, cols], sem.at[n]))
                        n += 1
                    first += 1
            for copy in copies:
                copy.start()
            for copy in copies:
                copy.wait()
        kernel(*weights, *own)
    return run


def weight_call(kernel, n, weights, ins, outs, name, flops, **more):
    plans = [[(a.shape[0], there, here, columns) for a, _, there, here, columns in w] for _, w in weights]
    operands = [(piece[0], "raw") for _, w in weights for piece in w]
    operands += [(jnp.concatenate([piece[1] for piece in w], 1), "scalars") for _, w in weights] + list(ins)
    scratch = []
    for width, w in weights:
        rows = sum(a.shape[0] * a.shape[1] * columns for a, _, _, _, columns in w) // width
        scratch.append(pltpu.VMEM((rows, width), BF))
        scratch.append(pltpu.SemaphoreType.DMA((sum(piece[0].shape[0] for piece in w),)))
    if "alias" in more:
        more["alias"] = {len(operands) - len(ins) + k: v for k, v in more["alias"].items()}
    return call(weighted(kernel, plans), n, operands, outs, name, flops * n * SP, scratch, **more)


def gradient_kernel(rows, steps, relative, spots, place_ref, l_ref, r_ref, *rest):
    outs, stage, sems = rest[:spots], rest[spots], rest[spots + 1]
    i, j = pl.program_id(0), pl.program_id(1)
    step = i * pl.num_programs(1) + j
    block, width = stage.shape[1], stage.shape[2]
    per = block // rows

    def copy(slot, t, out, at, cols):
        return pltpu.make_async_copy(stage.at[slot, t * rows:(t + 1) * rows, :], out.at[at, :, cols], sems.at[slot, t])

    def drain(slot):
        for t in range(per):
            copy(slot, t, outs[0], 0, pl.ds(0, width)).wait()

    slot = lax.rem(step, 2)

    @pl.when(step >= 2)
    def _():
        drain(slot)
    stage[slot] = lax.dot_general(l_ref[...], r_ref[...], (((0,), (0,)), ((), ())), preferred_element_type=F32).astype(BF)
    cols = pl.ds(pl.multiple_of(j * width, 128), width)
    for t in range(per):
        owner = i * per + t
        if not relative:
            copy(slot, t, outs[0], owner, cols).start()
            continue
        core = lax.rem(owner, 2) ^ place_ref[1]
        x = lax.rem(owner // 2, 2) ^ place_ref[0]
        z = owner // 4

        @pl.when(core == 1)
        def _():
            copy(slot, t, outs[0], x * (outs[0].shape[0] // 2) + z, cols).start()

        @pl.when(jnp.logical_and(core == 0, x == 0))
        def _():
            copy(slot, t, outs[1], z, cols).start()

        @pl.when(jnp.logical_and(core == 0, x == 1))
        def _():
            copy(slot, t, outs[2], z, cols).start()

    @pl.when(step == steps - 1)
    def _():
        drain(slot)
        if steps > 1:
            drain(1 - slot)


def weight_gradient(left, right, owners, place, relative, name, first=0, width=None):
    depth = left.shape[0] * left.shape[1]
    left, right = left.reshape(depth, -1), right.reshape(depth, -1)
    block, cols, width = 640, 1280, width or right.shape[1]
    if not relative:
        owners = left.shape[1] // block
    rows = left.shape[1] // owners
    steps = (left.shape[1] // block) * (width // cols)
    if relative:
        shapes = [sds(owners // 2, rows, width), sds(owners // 4, rows, width), sds(owners // 4, rows, width)]
    else:
        shapes = [sds(owners, rows, width)]

    def kernel(*refs):
        gradient_kernel(rows, steps, relative, len(shapes), *refs)

    return pl.pallas_call(
        kernel,
        grid=(left.shape[1] // block, width // cols),
        in_specs=[
            pl.BlockSpec(memory_space=pltpu.SMEM),
            pl.BlockSpec((depth, block), lambda i, j: (0, i)),
            pl.BlockSpec((depth, cols), lambda i, j: (0, j + first // cols)),
        ],
        out_specs=[pl.BlockSpec(memory_space=pl.ANY)] * len(shapes),
        out_shape=shapes,
        scratch_shapes=[pltpu.VMEM((2, block, cols), BF), pltpu.SemaphoreType.DMA((2, block // rows))],
        compiler_params=pltpu.CompilerParams(vmem_limit_bytes=60 << 20),
        cost_estimate=cost(2.5 * depth * left.shape[1] * width, [left, right] + shapes),
        name=name,
    )(place, left, right)


SWAP = [(0, 1), (1, 0)]


def row(vector):
    return vector.reshape(1, -1).astype(F32)


def after(value, *others):
    return lax.optimization_barrier((value, others))[0]


def both_groups(shard):
    if lax.axis_size("dp") != 2:
        return lax.psum(shard, "dp").astype(F32)
    return shard.astype(F32) + lax.ppermute(shard, "dp", SWAP).astype(F32)


class Whole:
    def __init__(self, owners):
        self.owners, self.mine, self.relative = owners, jnp.zeros((2,), jnp.int32), False

    def gather_small(self, vector):
        return lax.all_gather(vector.reshape(1, -1), "fsdp", axis=0, tiled=True)

    def gather(self, w):
        return [(lax.all_gather(w, "fsdp", axis=0, tiled=True)[None], jnp.zeros((2, 1), jnp.int32))]

    def first_stage(self, parts, *before):
        return parts

    def second_stage(self, parts, *before):
        return parts

    def third_stage(self, parts):
        whole = parts[0].reshape(-1, parts[0].shape[2])
        return lax.psum_scatter(whole, "fsdp", scatter_dimension=0, tiled=True)

    def scatter_small(self, shares):
        return lax.psum(lax.psum_scatter(shares, "fsdp", scatter_dimension=0, tiled=True)[0], "dp")


class Split:
    relative = True

    def __init__(self, owners):
        self.owners, self.count = owners, owners // 4
        self.mine = jnp.stack([lax.axis_index("x"), lax.axis_index("core")]).astype(jnp.int32)
        self.z = jnp.arange(self.count, dtype=jnp.int32)

    def gather(self, w):
        return [(lax.all_gather(w, ("z", "x", "core"), axis=0, tiled=True)[None], jnp.zeros((2, 1), jnp.int32))]

    def gather_small(self, vector):
        rows = vector.reshape(1, -1)

        def double(rows, axis, step, other):
            got = lax.ppermute(rows, axis, other)
            low = lax.rem(lax.axis_index(axis) // step, 2) == 0
            return jnp.concatenate([jnp.where(low, rows, got), jnp.where(low, got, rows)], 0)
        rows = double(rows, "core", 1, SWAP)
        rows = double(rows, "x", 1, SWAP)
        step = 1
        while step < self.count:
            rows = double(rows, "z", step, [(i, i ^ step) for i in range(self.count)])
            step *= 2
        return rows

    def first_stage(self, parts, *before):
        send, keep, pass_on = parts
        half = send.shape[0] // 2
        got = lax.ppermute(send, "core", SWAP)
        return after(pass_on, *before) + got[half:], keep, got

    def second_stage(self, parts, *before):
        passed, keep, got = parts
        half, keep = got.shape[0] // 2, after(keep, *before)
        got_x = lax.ppermute(passed, "x", SWAP)
        return (keep.astype(F32) + got[:half].astype(F32) + got_x.astype(F32)).astype(BF)

    def third_stage(self, total):
        return lax.psum_scatter(total, "z", scatter_dimension=0, tiled=True)[0]

    def scatter_small(self, shares):
        shares = shares.reshape(self.count, 2, 2, -1)

        def halve(rows, axis, here):
            kept = lax.dynamic_index_in_dim(rows, here, axis, keepdims=False)
            return kept, lax.dynamic_index_in_dim(rows, 1 - here, axis, keepdims=False)
        kept, sent = halve(shares, 2, self.mine[1])
        shares = kept + lax.ppermute(sent, "core", SWAP)
        kept, sent = halve(shares, 1, self.mine[0])
        shares = kept + lax.ppermute(sent, "x", SWAP)
        step = self.count // 2
        while step:
            shares = shares.reshape(2, step, -1)
            kept, sent = halve(shares, 0, lax.rem(lax.axis_index("z") // step, 2))
            shares = kept + lax.ppermute(sent, "z", [(i, i ^ step) for i in range(self.count)])
            step //= 2
        shares = shares.reshape(-1)
        if lax.axis_size("dp") != 2:
            return lax.psum(shares, "dp")
        return shares + lax.ppermute(shares, "dp", SWAP)


def row(vector):
    return vector.reshape(1, -1).astype(F32)


def columns(pieces, there, here, width):
    return [(a, places, there, here, width) for a, places in pieces]


def layer(links, images, cotangent, w_qkv, w_out, w_up, w_down, *vectors):
    n, owners = images.shape[0], links.owners

    sizes = [v.shape[0] for v in vectors]
    small = links.gather_small(jnp.concatenate(vectors))
    whole, first = [], 0
    for size in sizes:
        whole.append(row(small[:, first:first + size]))
        first += size
    b_qv, b_out, b_up, b_down, gain_one, shift_one, gain_two, shift_two = whole

    def image(a):
        return (a, "image")

    def fixed(a):
        return (a, "whole")

    def rows(*shape, dtype=BF):
        return (sds(n, *shape, dtype=dtype), "image")

    def sums(width):
        return (sds(8, width, dtype=F32), "sum")

    def gradient(left, right, name, first=0, width=None):
        return weight_gradient(left, right, owners, links.mine, links.relative, name, first, width)

    g_qkv = links.gather(w_qkv)
    full_qkv = columns(g_qkv, 0, 0, 3 * D)
    normed_one, cpad, s_down = call(
        prepare_kernel, n, [image(images), image(cotangent), fixed(gain_one), fixed(shift_one)],
        [rows(SP, D), rows(SP, D), sums(D)], "prepare", 8 * n * SP * D * 50)
    g_middle = links.gather(after(jnp.concatenate([w_out, w_up], 1), normed_one))
    full_out, full_up = columns(g_middle, 0, 0, D), columns(g_middle, D, 0, FF)
    bias = jnp.concatenate([b_qv[:, :D], jnp.zeros((1, D), F32), b_qv[:, D:]], 1)
    packed, = weight_call(
        qkv_kernel, n, [(3 * D, full_qkv)], [image(normed_one), fixed(bias)], [rows(SP, 3 * D)], "qkv", 2.5 * D * 3 * D)
    full_down = columns(links.gather(after(w_down, packed)), 0, 0, D)
    mixed, logsum = call(
        attention_kernel, n, [image(packed)], [rows(SP, D), rows(H, SP, dtype=F32)], "attention", 1e5 * n * SP * H)
    hidden, normed_two = weight_call(
        out_kernel, n, [(D, full_out)],
        [image(images), image(mixed), fixed(b_out), fixed(gain_two), fixed(shift_two)],
        [rows(SP, D, dtype=F32), rows(SP, D)], "out", 3 * D * D)
    active, slope = weight_call(
        up_kernel, n, [(FF, full_up)], [image(normed_two), fixed(b_up)], [rows(SP, FF), rows(SP, FF)], "up", 4 * D * FF)

    p_down = gradient(active, cpad, "g_down")
    result, = weight_call(
        down_kernel, n, [(D, full_down)],
        [image(after(active, p_down)), image(hidden), fixed(b_down)], [rows(SEQ, D, dtype=F32)], "down", 2.5 * D * FF)
    p_down = links.first_stage(p_down, result)
    d_inner, s_up = weight_call(
        down_back_kernel, n, [(D, full_down)], [image(after(cpad, result, p_down[0])), image(slope)],
        [rows(SP, FF), sums(FF)], "down_back", 3 * D * FF)
    p_up = gradient(normed_two, d_inner, "g_up_low", 0, FF // 2)
    p_up2 = gradient(normed_two, after(d_inner, p_up), "g_up_high", FF // 2, FF // 2)
    p_up = links.first_stage(p_up, p_up2)
    p_down = links.second_stage(p_down, p_up2)
    d_hidden, d_hidden_b, d_mixed, s_gain_two, s_shift_two, s_out = weight_call(
        up_back_kernel, n, [(FF, full_up), (D, full_out)],
        [image(after(d_inner, p_up2, p_up[0], p_down)), image(hidden), image(cpad), fixed(gain_two)],
        [rows(SP, D, dtype=F32), rows(SP, D), rows(SP, D), sums(D), sums(D), sums(D)], "up_back", 3 * D * (D + FF))
    p_down = links.third_stage(p_down)
    p_up2 = links.first_stage(p_up2, d_hidden_b)
    p_up = links.second_stage(p_up, d_hidden_b)
    p_out = gradient(mixed, after(d_hidden_b, p_up2[0], p_up, p_down), "g_out")
    p_up = links.third_stage(p_up)
    d_packed, s_qv = call(
        attention_back_kernel, n, [image(packed), image(mixed), image(after(d_mixed, p_out)), image(logsum)],
        [rows(SP, 3 * D), sums(2 * D)], "attention_back", 1.4e5 * n * SP * H)
    g_down = both_groups(after(p_down, d_packed))
    p_out = links.first_stage(p_out, d_packed)
    p_up2 = links.second_stage(p_up2, d_packed)
    p_q = gradient(normed_one, after(d_packed, p_out[0], p_up2, p_up), "g_q", 0, D)
    p_up2 = links.third_stage(p_up2)
    p_k = gradient(normed_one, after(d_packed, p_q), "g_k", D, D)
    p_q = links.first_stage(p_q, p_k)
    p_v = gradient(normed_one, after(d_packed, p_k, p_q[0]), "g_v", 2 * D, D)
    p_k = links.first_stage(p_k, p_v)
    p_out = links.second_stage(p_out, p_v)

    def qkv_back(first, d_packed, more):
        return weight_call(
            qkv_back_kernel, n // 2, [(3 * D, full_qkv)],
            [image(d_packed), image(images), image(d_hidden), fixed(gain_one)] + [(a, "raw") for a in more],
            [rows(SEQ, D, dtype=F32), sums(D), sums(D)], "qkv_back", 3 * D * 3 * D,
            first=first, alias={4: 0} if more else {})
    d_images, s_gain_one, s_shift_one = qkv_back(0, after(d_packed, p_v, p_k[0], p_out), ())
    g_up = both_groups(after(p_up, d_images))
    p_v = links.first_stage(p_v, d_images)
    p_q = links.second_stage(p_q, d_images)
    p_out = links.third_stage(after(p_out, p_up2, d_images))
    d_images, more_gain, more_shift = qkv_back(n // 2, after(d_packed, p_v[0], p_q, p_up2), (d_images,))
    p_q = links.third_stage(p_q)
    p_k = links.third_stage(links.second_stage(p_k, d_images))
    p_v = links.third_stage(links.second_stage(p_v, d_images))
    s_gain_one, s_shift_one = s_gain_one + more_gain, s_shift_one + more_shift
    g_up2, g_out, g_q, g_k, g_v = [both_groups(after(p, d_images)) for p in (p_up2, p_out, p_q, p_k, p_v)]
    g_up = jnp.concatenate([g_up, g_up2], 1)

    parts = [s_qv, s_out, s_up, s_down, s_gain_one, s_shift_one, s_gain_two, s_shift_two]
    share = links.scatter_small(jnp.concatenate([jnp.sum(s, 0).reshape(owners, -1) for s in parts], 1))
    small_grads, first = [], 0
    for size in sizes:
        small_grads.append(share[first:first + size])
        first += size
    return (result, d_images, jnp.concatenate([g_q, g_k, g_v], 1), g_out, g_up, g_down, *small_grads)


def solution(mesh):
    dp, owners = mesh.shape["dp"], mesh.shape["fsdp"]
    kind, fsdp = Whole, ("fsdp",)
    if dp == 2 and owners % 4 == 0 and (D // owners) % 16 == 0:
        kind, fsdp = Split, ("z", "x", "core")
        mesh = Mesh(mesh.devices.reshape(dp, owners // 4, 2, 2), ("dp",) + fsdp)
    images, matrix, vector = P(("dp",) + fsdp, None, None), P(fsdp, None), P(fsdp)
    specs = (images,) * 2 + (matrix,) * 4 + (vector,) * 8

    def run(*args):
        return layer(kind(owners), *args)

    return jax.shard_map(run, mesh=mesh, in_specs=specs, out_specs=specs, check_vma=False)
```

```python
import math

import jax
import jax.numpy as jnp
from jax import lax
from jax.experimental import pallas as pl
from jax.experimental.pallas import tpu as pltpu
from jax.sharding import Mesh
from jax.sharding import PartitionSpec as P

D = 1280
H = 16
HD = 80
FF = 5120
SEQ = 257
SP = 264
GROUP = 8
GW = GROUP * HD
EPS = 1e-06
SCALE = HD ** (-0.5)
NT = (((1,), (1,)), ((), ()))
BF = jnp.bfloat16
F32 = jnp.float32


def dot_nt(left, right):
    return lax.dot_general(left, right, NT, preferred_element_type=F32)


def dot_nn(left, right):
    return jnp.dot(left, right, preferred_element_type=F32)


def pad_rows(rows):
    return jnp.concatenate([rows, jnp.zeros((SP - SEQ, rows.shape[1]), rows.dtype)], 0)


def fold_rows(rows):
    return jnp.sum(rows.reshape(rows.shape[0] // 8, 8, rows.shape[1]), 0)


def standardize(rows):
    centered = rows - jnp.mean(rows, -1, keepdims=True)
    inverse = lax.rsqrt(jnp.mean(centered * centered, -1, keepdims=True) + EPS)
    return centered * inverse, inverse


def norm_gradient(e, xhat, inverse, gain):
    scaled = e * gain
    first = jnp.mean(scaled, -1, keepdims=True)
    second = jnp.mean(scaled * xhat, -1, keepdims=True)
    return inverse * (scaled - first - xhat * second)


def cost(flops, arrays):
    moved = sum(math.prod(a.shape) * a.dtype.itemsize for a in arrays)
    return pl.CostEstimate(flops=int(flops), transcendentals=0, bytes_accessed=moved)


def grid_call(kernel, grid, ins, outs, name, flops=0, scratch=()):
    return pl.pallas_call(
        kernel,
        grid=grid,
        in_specs=[spec for _, spec in ins],
        out_specs=[spec for _, spec in outs],
        out_shape=[a for a, _ in outs],
        scratch_shapes=list(scratch),
        compiler_params=pltpu.CompilerParams(vmem_limit_bytes=62 << 20),
        cost_estimate=cost(flops, [a for a, _ in ins] + [a for a, _ in outs]),
        name=name,
    )(*[a for a, _ in ins])


def whole(a):
    return a, pl.BlockSpec(tuple(a.shape), lambda *at: (0,) * len(a.shape), pipeline_mode=pl.Buffered(1))


def total(a):
    return a, pl.BlockSpec(tuple(a.shape), lambda *at: (0,) * len(a.shape))


def untouched(a):
    return a, pl.BlockSpec(memory_space=pl.ANY)


def call(kernel, n, ins, outs, name, flops=0, scratch=()):
    def specs(pairs):
        for a, kind in pairs:
            if kind == "image":
                kind = pl.BlockSpec((1,) + tuple(a.shape[1:]), lambda i, last=len(a.shape) - 1: (i,) + (0,) * last)
            yield a, kind
    return grid_call(kernel, (n,), list(specs(ins)), list(specs(outs)), name, flops, scratch)


def accumulate(ref, value):
    @pl.when(pl.program_id(0) == 0)
    def _():
        ref[...] = jnp.zeros_like(ref)
    ref[...] += value


def prepare_kernel(x_ref, c_ref, gain_ref, shift_ref, normed_ref, xpad_ref, cpad_ref, sum_ref):
    x = x_ref[0].astype(F32)
    xhat, _ = standardize(x)
    normed = xhat * gain_ref[...] + shift_ref[...]
    normed_ref[0] = pad_rows(normed).astype(BF)
    xpad_ref[0] = pad_rows(x).astype(BF)
    c = pad_rows(c_ref[0].astype(F32))
    cpad_ref[0] = c.astype(BF)
    accumulate(sum_ref, fold_rows(c))


def flat(ref):
    return ref[...].reshape(ref.shape[0] * ref.shape[1], ref.shape[2])


def qkv_kernel(w_ref, normed_ref, bias_ref, packed_ref):
    out = dot_nn(flat(normed_ref), w_ref[...]) + bias_ref[...]
    packed_ref[...] = out.astype(BF).reshape(packed_ref.shape)


def drop_tail(rows):
    tail = rows[SP - 8:]
    keep = lax.broadcasted_iota(jnp.int32, tail.shape, 0) < SEQ - (SP - 8)
    return jnp.concatenate([rows[:SP - 8], jnp.where(keep, tail, 0.0)], 0)


def attention_kernel(packed_ref, mixed_ref, lse_ref):
    def group(g, carry):
        base = g * GW
        here = pl.ds(pl.multiple_of(base, 128), GW)
        queries, keys, values = [
            packed_ref[0, :, pl.ds(pl.multiple_of(part * D + base, 128), GW)] for part in range(3)]
        values_t = values.astype(F32).T.astype(BF)
        outs, lses = [], []
        for j in range(GROUP):
            head = slice(j * HD, (j + 1) * HD)
            s = dot_nt(keys[:, head], queries[:, head])
            tail = s[SP - 8:]
            keep = lax.broadcasted_iota(jnp.int32, tail.shape, 0) < SEQ - (SP - 8)
            s = jnp.concatenate([s[:SP - 8], jnp.where(keep, tail, -1e30)], 0) * SCALE
            top = jnp.max(s, 0, keepdims=True)
            e = jnp.exp(s - top)
            total = jnp.sum(e, 0, keepdims=True)
            o = dot_nn(values_t[head], e.astype(BF)) * (1.0 / total)
            outs.append(o)
            lses.append(top + jnp.log(total))
        mixed_ref[0, :, pl.ds(pl.multiple_of(base, 128), GW)] = jnp.concatenate(outs, 0).T.astype(BF)
        lse_ref[0, pl.ds(pl.multiple_of(g * GROUP, 8), GROUP), :] = jnp.concatenate(lses, 0)
        return carry
    lax.fori_loop(0, H // GROUP, group, 0)


def out_kernel(w_ref, x_ref, mixed_ref, bias_ref, gain_ref, shift_ref, hidden_ref, normed_ref):
    hidden = flat(x_ref).astype(F32) + dot_nn(flat(mixed_ref), w_ref[...]) + bias_ref[...]
    hidden_ref[...] = hidden.reshape(hidden_ref.shape)
    xhat, _ = standardize(hidden)
    normed = xhat * gain_ref[...] + shift_ref[...]
    keep = lax.rem(lax.broadcasted_iota(jnp.int32, normed.shape, 0), SP) < SEQ
    normed_ref[...] = jnp.where(keep, normed, 0.0).astype(BF).reshape(normed_ref.shape)


def up_kernel(w_ref, normed_ref, bias_ref, active_ref, slope_ref):
    u = dot_nn(flat(normed_ref), w_ref[...]) + bias_ref[...]
    cdf = 0.5 * (1.0 + lax.erf(u * 0.7071067811865476))
    active_ref[...] = (u * cdf).astype(BF).reshape(active_ref.shape)
    slope_ref[...] = (cdf + u * jnp.exp(-0.5 * u * u) * 0.3989422804014327).astype(BF).reshape(slope_ref.shape)


def interleave(rows, out_ref, stage_ref, sems):
    image, last = pl.program_id(0), pl.num_programs(0) - 1
    tiles = stage_ref.shape[0]
    step = stage_ref.shape[1] // SEQ
    for k in range(tiles):
        stage_ref[k, pl.ds(image, SEQ, stride=step), :] = rows[:SEQ, k * 128:(k + 1) * 128]

    @pl.when(image == last)
    def _():
        copies = [pltpu.make_async_copy(stage_ref.at[k], out_ref.at[:, k * 128:(k + 1) * 128], sems.at[k]) for k in range(tiles)]
        for copy in copies:
            copy.start()
        for copy in copies:
            copy.wait()


def down_kernel(w_ref, active_ref, hidden_ref, bias_ref, result_ref, stage_ref, sems):
    result = hidden_ref[0] + dot_nn(active_ref[0], w_ref[...]) + bias_ref[...]
    interleave(result, result_ref, stage_ref, sems)


def down_back_kernel(w_ref, c_ref, slope_ref, dinner_ref, sum_ref):
    d = dot_nt(flat(c_ref), w_ref[...]) * flat(slope_ref).astype(F32)
    dinner_ref[...] = d.astype(BF).reshape(dinner_ref.shape)

    @pl.when(pl.program_id(1) == 0)
    def _():
        sum_ref[...] = jnp.zeros_like(sum_ref)
    sum_ref[...] += fold_rows(d)


def up_back_kernel(w_up_ref, dinner_ref, w_out_ref, hidden_ref, c_ref, gain_ref,
                   dhidden_ref, dhidden_b_ref, dmixed_ref, sum_gain_ref, sum_shift_ref, sum_out_ref, acc_ref):
    i, k = pl.program_id(0), pl.program_id(1)

    @pl.when(k == 0)
    def _():
        acc_ref[...] = dot_nt(flat(dinner_ref), w_up_ref[...])

    @pl.when(k > 0)
    def _():
        acc_ref[...] += dot_nt(flat(dinner_ref), w_up_ref[...])

    @pl.when(jnp.logical_and(i == 0, k == 0))
    def _():
        for ref in (sum_gain_ref, sum_shift_ref, sum_out_ref):
            ref[...] = jnp.zeros_like(ref)

    @pl.when(k == pl.num_programs(1) - 1)
    def _():
        for image in range(dhidden_ref.shape[0]):
            e = acc_ref[image * SP:(image + 1) * SP]
            xhat, inverse = standardize(hidden_ref[image])
            dhidden = c_ref[image].astype(F32) + norm_gradient(e, xhat, inverse, gain_ref[...])
            dhidden_ref[image] = dhidden
            dhidden_b = dhidden.astype(BF)
            dhidden_b_ref[image] = dhidden_b
            dmixed_ref[image] = dot_nt(dhidden_b, w_out_ref[...]).astype(BF)
            sum_gain_ref[...] += fold_rows(e * xhat)
            sum_shift_ref[...] += fold_rows(e)
            sum_out_ref[...] += fold_rows(dhidden)


def attention_back_kernel(packed_ref, mixed_ref, dmixed_ref, lse_ref, dpacked_ref, sum_ref):
    @pl.when(pl.program_id(0) == 0)
    def _():
        sum_ref[...] = jnp.zeros_like(sum_ref)

    def group(g, carry):
        base = g * GW
        here = pl.ds(pl.multiple_of(base, 128), GW)
        queries, keys, values = [
            packed_ref[0, :, pl.ds(pl.multiple_of(part * D + base, 128), GW)] for part in range(3)]
        grads = dmixed_ref[0, :, here]
        product = (grads.astype(F32) * mixed_ref[0, :, here].astype(F32)).T
        keys_t = keys.astype(F32).T.astype(BF)
        lse = lse_ref[0, pl.ds(pl.multiple_of(g * GROUP, 8), GROUP), :]
        dq, dk, dv = [], [], []
        for j in range(GROUP):
            head = slice(j * HD, (j + 1) * HD)
            q, k, v, dm = queries[:, head], keys[:, head], values[:, head], grads[:, head]
            delta = jnp.sum(product[head], 0, keepdims=True)
            p = drop_tail(jnp.exp(dot_nt(k, q) * SCALE - lse[j:j + 1]))
            dv.append(dot_nn(p.astype(BF), dm))
            ds = (p * (dot_nt(v, dm) - delta) * SCALE).astype(BF)
            dk.append(dot_nn(ds, q))
            dq.append(dot_nn(keys_t[head], ds))
        dq = jnp.concatenate(dq, 0).T
        dk = jnp.concatenate(dk, 1)
        dv = jnp.concatenate(dv, 1)
        def out(part):
            return pl.ds(pl.multiple_of(part * D + base, 128), GW)
        keep = lax.broadcasted_iota(jnp.int32, dq.shape, 0) < SEQ
        dq = jnp.where(keep, dq, 0.0)
        dpacked_ref[0, :, out(0)] = dq.astype(BF)
        dpacked_ref[0, :, out(1)] = dk.astype(BF)
        dpacked_ref[0, :, out(2)] = dv.astype(BF)
        sum_ref[:, out(0)] += fold_rows(dq)
        sum_ref[:, out(1)] += fold_rows(dv)
        return carry
    lax.fori_loop(0, H // GROUP, group, 0)


def qkv_back_kernel(w_ref, dpacked_ref, x_ref, dhidden_ref, gain_ref,
                    dimages_ref, sum_gain_ref, sum_shift_ref, stage_ref, sems):
    e = dot_nt(dpacked_ref[0], w_ref[...])
    xhat, inverse = standardize(x_ref[0].astype(F32))
    dimages = dhidden_ref[0] + norm_gradient(e, xhat, inverse, gain_ref[...])
    interleave(dimages, dimages_ref, stage_ref, sems)
    accumulate(sum_gain_ref, fold_rows(e * xhat))
    accumulate(sum_shift_ref, fold_rows(e))


def sds(*shape, dtype=BF):
    return jax.ShapeDtypeStruct(shape, dtype)


def gradient_kernel(rows, steps, relative, spots, place_ref, l_ref, r_ref, *rest):
    outs, stage, sems = rest[:spots], rest[spots], rest[spots + 1]
    i, j = pl.program_id(0), pl.program_id(1)
    step = i * pl.num_programs(1) + j
    block, width = stage.shape[1], stage.shape[2]
    per = block // rows

    def copy(slot, t, out, at, cols):
        return pltpu.make_async_copy(stage.at[slot, t * rows:(t + 1) * rows, :], out.at[at, :, cols], sems.at[slot, t])

    def drain(slot):
        for t in range(per):
            copy(slot, t, outs[0], 0, pl.ds(0, width)).wait()

    slot = lax.rem(step, 2)

    @pl.when(step >= 2)
    def _():
        drain(slot)
    stage[slot] = lax.dot_general(l_ref[...], r_ref[...], (((0,), (0,)), ((), ())), preferred_element_type=F32).astype(BF)
    cols = pl.ds(pl.multiple_of(j * width, 128), width)
    for t in range(per):
        owner = i * per + t
        if not relative:
            copy(slot, t, outs[0], owner, cols).start()
            continue
        core = lax.rem(owner, 2) ^ place_ref[1]
        x = lax.rem(owner // 2, 2) ^ place_ref[0]
        z = owner // 4

        @pl.when(core == 1)
        def _():
            copy(slot, t, outs[0], x * (outs[0].shape[0] // 2) + z, cols).start()

        @pl.when(jnp.logical_and(core == 0, x == 0))
        def _():
            copy(slot, t, outs[1], z, cols).start()

        @pl.when(jnp.logical_and(core == 0, x == 1))
        def _():
            copy(slot, t, outs[2], z, cols).start()

    @pl.when(step == steps - 1)
    def _():
        drain(slot)
        if steps > 1:
            drain(1 - slot)


def weight_gradient(left, right, owners, place, relative, name, first=0, width=None):
    depth = left.shape[0] * left.shape[1]
    left, right = left.reshape(depth, -1), right.reshape(depth, -1)
    block, cols, width = 640, 1280, width or right.shape[1]
    if not relative:
        owners = left.shape[1] // block
    rows = left.shape[1] // owners
    steps = (left.shape[1] // block) * (width // cols)
    if relative:
        shapes = [sds(owners // 2, rows, width), sds(owners // 4, rows, width), sds(owners // 4, rows, width)]
    else:
        shapes = [sds(owners, rows, width)]

    def kernel(*refs):
        gradient_kernel(rows, steps, relative, len(shapes), *refs)

    return pl.pallas_call(
        kernel,
        grid=(left.shape[1] // block, width // cols),
        in_specs=[
            pl.BlockSpec(memory_space=pltpu.SMEM),
            pl.BlockSpec((depth, block), lambda i, j: (0, i)),
            pl.BlockSpec((depth, cols), lambda i, j: (0, j + first // cols)),
        ],
        out_specs=[pl.BlockSpec(memory_space=pl.ANY)] * len(shapes),
        out_shape=shapes,
        scratch_shapes=[pltpu.VMEM((2, block, cols), BF), pltpu.SemaphoreType.DMA((2, block // rows))],
        compiler_params=pltpu.CompilerParams(vmem_limit_bytes=60 << 20),
        cost_estimate=cost(2.5 * depth * left.shape[1] * width, [left, right] + shapes),
        name=name,
    )(place, left, right)


SWAP = [(0, 1), (1, 0)]


def row(vector):
    return vector.reshape(1, -1).astype(F32)


def after(value, *others):
    return lax.optimization_barrier((value, others))[0]


def both_groups(shard):
    if lax.axis_size("dp") != 2:
        return lax.psum(shard, "dp").astype(F32)
    return shard.astype(F32) + lax.ppermute(shard, "dp", SWAP).astype(F32)


class Whole:
    def __init__(self, owners):
        self.owners, self.mine, self.relative = owners, jnp.zeros((2,), jnp.int32), False

    def gather_small(self, vector):
        return lax.all_gather(vector.reshape(1, -1), "fsdp", axis=0, tiled=True)

    def gather(self, w):
        return lax.all_gather(w, "fsdp", axis=0, tiled=True)

    def first_stage(self, parts, *before):
        return parts

    def second_stage(self, parts, *before):
        return parts

    def joined(self, parts):
        return (jnp.concatenate([p[0] for p in parts], 2),)

    def third_stage(self, parts):
        whole = parts[0].reshape(-1, parts[0].shape[2])
        return lax.psum_scatter(whole, "fsdp", scatter_dimension=0, tiled=True)

    def scatter_small(self, shares):
        return lax.psum(lax.psum_scatter(shares, "fsdp", scatter_dimension=0, tiled=True)[0], "dp")


class Split:
    relative = True

    def __init__(self, owners):
        self.owners, self.count = owners, owners // 4
        self.mine = jnp.stack([lax.axis_index("x"), lax.axis_index("core")]).astype(jnp.int32)
        self.z = jnp.arange(self.count, dtype=jnp.int32)

    def gather(self, w):
        return lax.all_gather(w, ("z", "x", "core"), axis=0, tiled=True)

    def gather_small(self, vector):
        rows = vector.reshape(1, -1)

        def double(rows, axis, step, other):
            got = lax.ppermute(rows, axis, other)
            low = lax.rem(lax.axis_index(axis) // step, 2) == 0
            return jnp.concatenate([jnp.where(low, rows, got), jnp.where(low, got, rows)], 0)
        rows = double(rows, "core", 1, SWAP)
        rows = double(rows, "x", 1, SWAP)
        step = 1
        while step < self.count:
            rows = double(rows, "z", step, [(i, i ^ step) for i in range(self.count)])
            step *= 2
        return rows

    def first_stage(self, parts, *before):
        send, keep, pass_on = parts
        half = send.shape[0] // 2
        got = lax.ppermute(send, "core", SWAP)
        return after(pass_on, *before) + got[half:], keep, got

    def second_stage(self, parts, *before):
        passed, keep, got = parts
        half, keep = got.shape[0] // 2, after(keep, *before)
        got_x = lax.ppermute(passed, "x", SWAP)
        return (keep.astype(F32) + got[:half].astype(F32) + got_x.astype(F32)).astype(BF)

    def joined(self, parts):
        return tuple(jnp.concatenate(a, 2) for a in zip(*parts))

    def third_stage(self, total):
        return lax.psum_scatter(total, "z", scatter_dimension=0, tiled=True)[0]

    def scatter_small(self, shares):
        shares = shares.reshape(self.count, 2, 2, -1)

        def halve(rows, axis, here):
            kept = lax.dynamic_index_in_dim(rows, here, axis, keepdims=False)
            return kept, lax.dynamic_index_in_dim(rows, 1 - here, axis, keepdims=False)
        kept, sent = halve(shares, 2, self.mine[1])
        shares = kept + lax.ppermute(sent, "core", SWAP)
        kept, sent = halve(shares, 1, self.mine[0])
        shares = kept + lax.ppermute(sent, "x", SWAP)
        step = self.count // 2
        while step:
            shares = shares.reshape(2, step, -1)
            kept, sent = halve(shares, 0, lax.rem(lax.axis_index("z") // step, 2))
            shares = kept + lax.ppermute(sent, "z", [(i, i ^ step) for i in range(self.count)])
            step //= 2
        shares = shares.reshape(-1)
        if lax.axis_size("dp") != 2:
            return lax.psum(shares, "dp")
        return shares + lax.ppermute(shares, "dp", SWAP)


def row(vector):
    return vector.reshape(1, -1).astype(F32)


def layer(links, images, cotangent, w_qkv, w_out, w_up, w_down, *vectors):
    n, owners = images.shape[0], links.owners

    sizes = [v.shape[0] for v in vectors]
    small = links.gather_small(jnp.concatenate(vectors))
    full, first = [], 0
    for size in sizes:
        full.append(row(small[:, first:first + size]))
        first += size
    b_qv, b_out, b_up, b_down, gain_one, shift_one, gain_two, shift_two = full

    def image(a):
        return (a, "image")

    def rows(*shape, dtype=BF):
        return (sds(n, *shape, dtype=dtype), "image")

    def sums(width):
        return total(sds(8, width, dtype=F32))

    def gradient(left, right, name, first=0, width=None):
        return weight_gradient(left, right, owners, links.mine, links.relative, name, first, width)

    def by_columns(kernel, weight, rows_in, others, outs, name, flops, sum_width=0):
        def cut(a):
            if len(a.shape) == 2:
                return a, pl.BlockSpec((a.shape[0], D), lambda j, i: (0, j))
            return a, pl.BlockSpec((4, SP, D), lambda j, i: (i, 0, j))
        results = [cut(a) for a in outs]
        return grid_call(
            kernel, (outs[0].shape[2] // D, n // 4),
            [weight, (rows_in, pl.BlockSpec((4, SP, D), lambda j, i: (i, 0, 0)))] + [cut(a) for a in others],
            results, name, flops * n * SP)

    full_qkv = links.gather(w_qkv)
    normed_one, xpad, cpad, s_down = call(
        prepare_kernel, n, [image(images), image(cotangent), whole(gain_one), whole(shift_one)],
        [rows(SP, D), rows(SP, D), rows(SP, D), sums(D)], "prepare", 8 * n * SP * D * 50)
    middle = links.gather(after(jnp.concatenate([w_up, w_out], 1), normed_one))
    full_out = middle, pl.BlockSpec((D, D), lambda *at: (0, FF // D), pipeline_mode=pl.Buffered(1))
    bias = jnp.concatenate([b_qv[:, :D], jnp.zeros((1, D), F32), b_qv[:, D:]], 1)
    packed, = by_columns(
        qkv_kernel, (full_qkv, pl.BlockSpec((D, D), lambda j, i: (0, j))), normed_one, [bias], [sds(n, SP, 3 * D)],
        "qkv", 2.5 * D * 3 * D)
    full_down = links.gather(after(w_down, packed))
    mixed, logsum = call(
        attention_kernel, n, [image(packed)], [rows(SP, D), rows(H, SP, dtype=F32)], "attention", 1e5 * n * SP * H)
    hidden, normed_two = call(
        out_kernel, n,
        [full_out, image(xpad), image(mixed), whole(b_out), whole(gain_two), whole(shift_two)],
        [rows(SP, D, dtype=F32), rows(SP, D)], "out", 3 * D * D * n * SP)
    active, slope = by_columns(
        up_kernel, (middle, pl.BlockSpec((D, D), lambda j, i: (0, j))), normed_two, [b_up], [sds(n, SP, FF)] * 2,
        "up", 4 * D * FF)

    p_down = gradient(active, cpad, "g_down")
    staging = [pltpu.VMEM((D // 128, SEQ * n, 128), F32), pltpu.SemaphoreType.DMA((D // 128,))]
    result, = call(
        down_kernel, n, [whole(full_down), image(after(active, p_down)), image(hidden), whole(b_down)],
        [untouched(sds(SEQ * n, D, dtype=F32))], "down", 2.5 * D * FF * n * SP, staging)
    p_down = links.first_stage(p_down, result)
    d_inner, s_up = by_columns(
        down_back_kernel, (full_down, pl.BlockSpec((D, D), lambda j, i: (j, 0))), after(cpad, result, p_down[0]), [slope],
        [sds(n, SP, FF), sds(8, FF, dtype=F32)], "down_back", 3 * D * FF)
    p_up = gradient(normed_two, d_inner, "g_up_low", 0, FF // 2)
    p_up2 = gradient(normed_two, after(d_inner, p_up), "g_up_high", FF // 2, FF // 2)
    p_up = links.first_stage(p_up, p_up2)
    p_down = links.second_stage(p_down, p_up2)

    def pair(a):
        return a, pl.BlockSpec((2,) + tuple(a.shape[1:]), lambda i, k: (i, 0, 0))
    d_hidden, d_hidden_b, d_mixed, s_gain_two, s_shift_two, s_out = grid_call(
        up_back_kernel, (n // 2, 2),
        [(middle, pl.BlockSpec((D, FF // 2), lambda i, k: (0, k))),
         (after(d_inner, p_up2, p_up[0], p_down), pl.BlockSpec((2, SP, FF // 2), lambda i, k: (i, 0, k))),
         full_out, pair(hidden), pair(cpad), whole(gain_two)],
        [pair(sds(n, SP, D, dtype=F32)), pair(sds(n, SP, D)), pair(sds(n, SP, D)), sums(D), sums(D), sums(D)],
        "up_back", 3 * D * (D + FF) * n * SP, [pltpu.VMEM((2 * SP, D), F32)])
    p_down = links.third_stage(p_down)
    p_up = links.second_stage(p_up, d_hidden_b)
    p_out = gradient(mixed, after(d_hidden_b, p_up, p_down), "g_out")
    p_up = links.third_stage(p_up)
    p_up2 = links.first_stage(p_up2, p_out)
    p_out = links.first_stage(p_out)
    rest = links.joined([p_up2, p_out])
    d_packed, s_qv = call(
        attention_back_kernel, n, [image(packed), image(mixed), image(after(d_mixed, rest[0])), image(logsum)],
        [rows(SP, 3 * D), sums(2 * D)], "attention_back", 1.4e5 * n * SP * H)
    g_down = both_groups(after(p_down, d_packed))
    rest = links.second_stage(rest, d_packed)
    p_qk = gradient(normed_one, after(d_packed, rest, p_up), "g_qk", 0, 2 * D)
    rest = links.third_stage(rest)
    p_v = gradient(normed_one, after(d_packed, p_qk), "g_v", 2 * D, D)
    p_qk = links.first_stage(p_qk, p_v)
    d_images, s_gain_one, s_shift_one = call(
        qkv_back_kernel, n,
        [whole(full_qkv), image(after(d_packed, p_v, p_qk[0], rest)), image(xpad), image(d_hidden), whole(gain_one)],
        [untouched(sds(SEQ * n, D, dtype=F32)), sums(D), sums(D)], "qkv_back", 3 * D * 3 * D * n * SP, staging)
    g_up = both_groups(after(p_up, p_qk[0]))
    p_v = links.first_stage(p_v, d_images)
    p_qk = links.second_stage(p_qk, d_images)
    p_v = links.second_stage(p_v, d_images, p_qk)
    p_qk = links.third_stage(p_qk)
    s_gain_one = after(s_gain_one, p_v)
    rest = both_groups(after(rest, p_qk))
    g_up2, g_out = rest[:, :FF // 2], rest[:, FF // 2:]
    p_v = links.third_stage(after(p_v, p_qk))
    g_qk, g_v = both_groups(p_qk), both_groups(p_v)
    result, d_images = [jnp.transpose(a.reshape(SEQ, n, D), (1, 0, 2)) for a in (result, d_images)]
    g_up = jnp.concatenate([g_up, g_up2], 1)

    parts = [s_qv, s_out, s_up, s_down, s_gain_one, s_shift_one, s_gain_two, s_shift_two]
    share = links.scatter_small(jnp.concatenate([jnp.sum(s, 0).reshape(owners, -1) for s in parts], 1))
    small_grads, first = [], 0
    for size in sizes:
        small_grads.append(share[first:first + size])
        first += size
    return (result, d_images, jnp.concatenate([g_qk, g_v], 1), g_out, g_up, g_down, *small_grads)


def solution(mesh):
    dp, owners = mesh.shape["dp"], mesh.shape["fsdp"]
    kind, fsdp = Whole, ("fsdp",)
    if dp == 2 and owners % 4 == 0 and (D // owners) % 16 == 0:
        kind, fsdp = Split, ("z", "x", "core")
        mesh = Mesh(mesh.devices.reshape(dp, owners // 4, 2, 2), ("dp",) + fsdp)
    images, matrix, vector = P(("dp",) + fsdp, None, None), P(fsdp, None), P(fsdp)
    specs = (images,) * 2 + (matrix,) * 4 + (vector,) * 8

    def run(*args):
        return layer(kind(owners), *args)

    return jax.shard_map(run, mesh=mesh, in_specs=specs, out_specs=specs, check_vma=False)
```

```python
import math

import jax
import jax.numpy as jnp
from jax import lax
from jax.experimental import pallas as pl
from jax.experimental.pallas import tpu as pltpu
from jax.sharding import Mesh
from jax.sharding import PartitionSpec as P

D = 1280
H = 16
HD = 80
FF = 5120
SEQ = 257
SP = 264
GROUP = 8
GW = GROUP * HD
EPS = 1e-06
SCALE = HD ** (-0.5)
NT = (((1,), (1,)), ((), ()))
BF = jnp.bfloat16
F32 = jnp.float32


def dot_nt(left, right):
    return lax.dot_general(left, right, NT, preferred_element_type=F32)


def dot_nn(left, right):
    return jnp.dot(left, right, preferred_element_type=F32)


def pad_rows(rows):
    return jnp.concatenate([rows, jnp.zeros((SP - SEQ, rows.shape[1]), rows.dtype)], 0)


def fold_rows(rows):
    return jnp.sum(rows.reshape(rows.shape[0] // 8, 8, rows.shape[1]), 0)


def standardize(rows):
    centered = rows - jnp.mean(rows, -1, keepdims=True)
    inverse = lax.rsqrt(jnp.mean(centered * centered, -1, keepdims=True) + EPS)
    return centered * inverse, inverse


def norm_gradient(e, xhat, inverse, gain):
    scaled = e * gain
    first = jnp.mean(scaled, -1, keepdims=True)
    second = jnp.mean(scaled * xhat, -1, keepdims=True)
    return inverse * (scaled - first - xhat * second)


def cost(flops, arrays):
    moved = sum(math.prod(a.shape) * a.dtype.itemsize for a in arrays)
    return pl.CostEstimate(flops=int(flops), transcendentals=0, bytes_accessed=moved)


def grid_call(kernel, grid, ins, outs, name, flops=0, scratch=()):
    return pl.pallas_call(
        kernel,
        grid=grid,
        in_specs=[spec for _, spec in ins],
        out_specs=[spec for _, spec in outs],
        out_shape=[a for a, _ in outs],
        scratch_shapes=list(scratch),
        compiler_params=pltpu.CompilerParams(vmem_limit_bytes=62 << 20),
        cost_estimate=cost(flops, [a for a, _ in ins] + [a for a, _ in outs]),
        name=name,
    )(*[a for a, _ in ins])


def whole(a):
    return a, pl.BlockSpec(tuple(a.shape), lambda *at: (0,) * len(a.shape), pipeline_mode=pl.Buffered(1))


def total(a):
    return a, pl.BlockSpec(tuple(a.shape), lambda *at: (0,) * len(a.shape))


def untouched(a):
    return a, pl.BlockSpec(memory_space=pl.ANY)


def call(kernel, n, ins, outs, name, flops=0, scratch=()):
    def specs(pairs):
        for a, kind in pairs:
            if kind == "image":
                kind = pl.BlockSpec((1,) + tuple(a.shape[1:]), lambda i, last=len(a.shape) - 1: (i,) + (0,) * last)
            yield a, kind
    return grid_call(kernel, (n,), list(specs(ins)), list(specs(outs)), name, flops, scratch)


def accumulate(ref, value):
    @pl.when(pl.program_id(0) == 0)
    def _():
        ref[...] = jnp.zeros_like(ref)
    ref[...] += value


def prepare_kernel(x_ref, c_ref, gain_ref, shift_ref, normed_ref, xpad_ref, cpad_ref, sum_ref):
    x = x_ref[0].astype(F32)
    xhat, _ = standardize(x)
    normed = xhat * gain_ref[...] + shift_ref[...]
    normed_ref[0] = pad_rows(normed).astype(BF)
    xpad_ref[0] = pad_rows(x).astype(BF)
    c = pad_rows(c_ref[0].astype(F32))
    cpad_ref[0] = c.astype(BF)
    accumulate(sum_ref, fold_rows(c))


def flat(ref):
    return ref[...].reshape(ref.shape[0] * ref.shape[1], ref.shape[2])


def qkv_kernel(w_ref, normed_ref, bias_ref, packed_ref):
    out = dot_nn(flat(normed_ref), w_ref[...]) + bias_ref[...]
    packed_ref[...] = out.astype(BF).reshape(packed_ref.shape)


def drop_tail(rows):
    tail = rows[SP - 8:]
    keep = lax.broadcasted_iota(jnp.int32, tail.shape, 0) < SEQ - (SP - 8)
    return jnp.concatenate([rows[:SP - 8], jnp.where(keep, tail, 0.0)], 0)


def attention_kernel(packed_ref, mixed_ref, lse_ref):
    def group(g, carry):
        base = g * GW
        here = pl.ds(pl.multiple_of(base, 128), GW)
        queries, keys, values = [
            packed_ref[0, :, pl.ds(pl.multiple_of(part * D + base, 128), GW)] for part in range(3)]
        values_t = values.astype(F32).T.astype(BF)
        outs, lses = [], []
        for j in range(GROUP):
            head = slice(j * HD, (j + 1) * HD)
            s = dot_nt(keys[:, head], queries[:, head])
            tail = s[SP - 8:]
            keep = lax.broadcasted_iota(jnp.int32, tail.shape, 0) < SEQ - (SP - 8)
            s = jnp.concatenate([s[:SP - 8], jnp.where(keep, tail, -1e30)], 0) * SCALE
            top = jnp.max(s, 0, keepdims=True)
            e = jnp.exp(s - top)
            total = jnp.sum(e, 0, keepdims=True)
            o = dot_nn(values_t[head], e.astype(BF)) * (1.0 / total)
            outs.append(o)
            lses.append(top + jnp.log(total))
        mixed_ref[0, :, pl.ds(pl.multiple_of(base, 128), GW)] = jnp.concatenate(outs, 0).T.astype(BF)
        lse_ref[0, pl.ds(pl.multiple_of(g * GROUP, 8), GROUP), :] = jnp.concatenate(lses, 0)
        return carry
    lax.fori_loop(0, H // GROUP, group, 0)


def out_kernel(w_ref, x_ref, mixed_ref, bias_ref, gain_ref, shift_ref, hidden_ref, normed_ref):
    hidden = flat(x_ref).astype(F32) + dot_nn(flat(mixed_ref), w_ref[...]) + bias_ref[...]
    hidden_ref[...] = hidden.reshape(hidden_ref.shape)
    xhat, _ = standardize(hidden)
    normed = xhat * gain_ref[...] + shift_ref[...]
    keep = lax.rem(lax.broadcasted_iota(jnp.int32, normed.shape, 0), SP) < SEQ
    normed_ref[...] = jnp.where(keep, normed, 0.0).astype(BF).reshape(normed_ref.shape)


def up_kernel(w_ref, normed_ref, bias_ref, active_ref, slope_ref):
    u = dot_nn(flat(normed_ref), w_ref[...]) + bias_ref[...]
    cdf = 0.5 * (1.0 + lax.erf(u * 0.7071067811865476))
    active_ref[...] = (u * cdf).astype(BF).reshape(active_ref.shape)
    slope_ref[...] = (cdf + u * jnp.exp(-0.5 * u * u) * 0.3989422804014327).astype(BF).reshape(slope_ref.shape)


def interleave(rows, out_ref, stage_ref, sems):
    image, last = pl.program_id(0), pl.num_programs(0) - 1
    tiles = stage_ref.shape[0]
    step = stage_ref.shape[1] // SEQ
    for k in range(tiles):
        stage_ref[k, pl.ds(image, SEQ, stride=step), :] = rows[:SEQ, k * 128:(k + 1) * 128]

    @pl.when(image == last)
    def _():
        copies = [pltpu.make_async_copy(stage_ref.at[k], out_ref.at[:, k * 128:(k + 1) * 128], sems.at[k]) for k in range(tiles)]
        for copy in copies:
            copy.start()
        for copy in copies:
            copy.wait()


def down_kernel(w_ref, active_ref, hidden_ref, bias_ref, result_ref, stage_ref, sems):
    result = hidden_ref[0] + dot_nn(active_ref[0], w_ref[...]) + bias_ref[...]
    interleave(result, result_ref, stage_ref, sems)


def down_back_kernel(w_ref, c_ref, slope_ref, dinner_ref, sum_ref):
    d = dot_nt(flat(c_ref), w_ref[...]) * flat(slope_ref).astype(F32)
    dinner_ref[...] = d.astype(BF).reshape(dinner_ref.shape)

    @pl.when(pl.program_id(1) == 0)
    def _():
        sum_ref[...] = jnp.zeros_like(sum_ref)
    sum_ref[...] += fold_rows(d)


def up_back_kernel(w_up_ref, dinner_ref, w_out_ref, hidden_ref, c_ref, gain_ref,
                   dhidden_ref, dhidden_b_ref, dmixed_ref, sum_gain_ref, sum_shift_ref, sum_out_ref, acc_ref):
    i, k = pl.program_id(0), pl.program_id(1)

    @pl.when(k == 0)
    def _():
        acc_ref[...] = dot_nt(flat(dinner_ref), w_up_ref[...])

    @pl.when(k > 0)
    def _():
        acc_ref[...] += dot_nt(flat(dinner_ref), w_up_ref[...])

    @pl.when(jnp.logical_and(i == 0, k == 0))
    def _():
        for ref in (sum_gain_ref, sum_shift_ref, sum_out_ref):
            ref[...] = jnp.zeros_like(ref)

    @pl.when(k == pl.num_programs(1) - 1)
    def _():
        for image in range(dhidden_ref.shape[0]):
            e = acc_ref[image * SP:(image + 1) * SP]
            xhat, inverse = standardize(hidden_ref[image])
            dhidden = c_ref[image].astype(F32) + norm_gradient(e, xhat, inverse, gain_ref[...])
            dhidden_ref[image] = dhidden
            dhidden_b = dhidden.astype(BF)
            dhidden_b_ref[image] = dhidden_b
            dmixed_ref[image] = dot_nt(dhidden_b, w_out_ref[...]).astype(BF)
            sum_gain_ref[...] += fold_rows(e * xhat)
            sum_shift_ref[...] += fold_rows(e)
            sum_out_ref[...] += fold_rows(dhidden)


def attention_back_kernel(packed_ref, mixed_ref, dmixed_ref, lse_ref, dpacked_ref, sum_ref):
    full = SEQ - 1

    @pl.when(pl.program_id(0) == 0)
    def _():
        sum_ref[...] = jnp.zeros_like(sum_ref)

    def group(g, carry):
        base = g * GW
        queries, keys, values = [
            packed_ref[0, :, pl.ds(pl.multiple_of(part * D + base, 128), GW)] for part in range(3)]
        here = pl.ds(pl.multiple_of(base, 128), GW)
        grads = dmixed_ref[0, :, here]
        product = grads.astype(F32) * mixed_ref[0, :, here].astype(F32)
        product_t = product[:full].T
        keys_t = keys.astype(F32).T
        keys_tb = keys_t[:, :full].astype(BF)
        lse = lse_ref[0, pl.ds(pl.multiple_of(g * GROUP, 8), GROUP), :]
        dq, dk, dv = [], [], []
        for j in range(GROUP):
            head = slice(j * HD, (j + 1) * HD)
            q, k, v, dm = queries[:full, head], keys[:, head], values[:, head], grads[:full, head]
            delta = jnp.sum(product_t[head], 0, keepdims=True)
            p = drop_tail(jnp.exp(dot_nt(k, q) * SCALE - lse[j:j + 1, :full]))
            dv.append(dot_nn(p.astype(BF), dm))
            ds = (p * (dot_nt(v, dm) - delta) * SCALE).astype(BF)
            dk.append(dot_nn(ds, q))
            dq.append(dot_nn(keys_tb[head], ds[:full])
                      + keys_t[head, full:full + 1] * ds[full:].astype(F32)[:1])
        dq = jnp.concatenate(dq, 0).T
        dk = jnp.concatenate(dk, 1)
        dv = jnp.concatenate(dv, 1)

        head_row = lax.broadcasted_iota(jnp.int32, (GROUP, GW), 0)
        lane = lax.broadcasted_iota(jnp.int32, (GROUP, GW), 1)
        mine = jnp.logical_and(lane >= head_row * HD, lane < (head_row + 1) * HD)
        diagonal = lax.broadcasted_iota(jnp.int32, (GROUP, GROUP), 0) == lax.broadcasted_iota(jnp.int32, (GROUP, GROUP), 1)

        def spread(rows):
            return jnp.where(mine, rows[full:].astype(F32)[:1], 0.0)

        def as_row(column):
            return jnp.sum(jnp.where(diagonal, column, 0.0), 0, keepdims=True)
        q, dm = spread(queries).astype(BF), spread(grads).astype(BF)
        delta = as_row(jnp.sum(spread(product), 1, keepdims=True))
        p = drop_tail(jnp.exp(dot_nt(keys, q) * SCALE - as_row(lse[:, full:full + 1])))
        ds = p * (dot_nt(values, dm) - delta) * SCALE
        dv = dv + dot_nn(p.astype(BF), dm)
        dk = dk + dot_nn(ds.astype(BF), q)
        ds_t = jnp.concatenate([ds, jnp.zeros((SP, 128 - GROUP), F32)], 1).T[:GROUP].astype(BF)
        dq_last = jnp.sum(jnp.where(mine, dot_nn(ds_t, keys), 0.0), 0, keepdims=True)
        tail = lax.broadcasted_iota(jnp.int32, (SP - full, GW), 0) == 0
        dq_last = jnp.where(tail, dq_last, 0.0)

        def out(part):
            return pl.ds(pl.multiple_of(part * D + base, 128), GW)
        dpacked_ref[0, :full, out(0)] = dq.astype(BF)
        dpacked_ref[0, full:, out(0)] = dq_last.astype(BF)
        dpacked_ref[0, :, out(1)] = dk.astype(BF)
        dpacked_ref[0, :, out(2)] = dv.astype(BF)
        sum_ref[:, out(0)] += fold_rows(dq) + dq_last
        sum_ref[:, out(1)] += fold_rows(dv)
        return carry
    lax.fori_loop(0, H // GROUP, group, 0)


def qkv_back_kernel(w_ref, dpacked_ref, x_ref, dhidden_ref, gain_ref,
                    dimages_ref, sum_gain_ref, sum_shift_ref, stage_ref, sems):
    e = dot_nt(dpacked_ref[0], w_ref[...])
    xhat, inverse = standardize(x_ref[0].astype(F32))
    dimages = dhidden_ref[0] + norm_gradient(e, xhat, inverse, gain_ref[...])
    interleave(dimages, dimages_ref, stage_ref, sems)
    accumulate(sum_gain_ref, fold_rows(e * xhat))
    accumulate(sum_shift_ref, fold_rows(e))


def sds(*shape, dtype=BF):
    return jax.ShapeDtypeStruct(shape, dtype)


def gradient_kernel(rows, steps, relative, spots, place_ref, l_ref, r_ref, *rest):
    outs, stage, sems = rest[:spots], rest[spots], rest[spots + 1]
    i, j = pl.program_id(0), pl.program_id(1)
    step = i * pl.num_programs(1) + j
    block, width = stage.shape[1], stage.shape[2]
    per = block // rows

    def copy(slot, t, out, at, cols):
        return pltpu.make_async_copy(stage.at[slot, t * rows:(t + 1) * rows, :], out.at[at, :, cols], sems.at[slot, t])

    def drain(slot):
        for t in range(per):
            copy(slot, t, outs[0], 0, pl.ds(0, width)).wait()

    slot = lax.rem(step, 2)

    @pl.when(step >= 2)
    def _():
        drain(slot)
    stage[slot] = lax.dot_general(l_ref[...], r_ref[...], (((0,), (0,)), ((), ())), preferred_element_type=F32).astype(BF)
    cols = pl.ds(pl.multiple_of(j * width, 128), width)
    for t in range(per):
        owner = i * per + t
        if not relative:
            copy(slot, t, outs[0], owner, cols).start()
            continue
        core = lax.rem(owner, 2) ^ place_ref[1]
        x = lax.rem(owner // 2, 2) ^ place_ref[0]
        z = owner // 4

        @pl.when(core == 1)
        def _():
            copy(slot, t, outs[0], x * (outs[0].shape[0] // 2) + z, cols).start()

        @pl.when(jnp.logical_and(core == 0, x == 0))
        def _():
            copy(slot, t, outs[1], z, cols).start()

        @pl.when(jnp.logical_and(core == 0, x == 1))
        def _():
            copy(slot, t, outs[2], z, cols).start()

    @pl.when(step == steps - 1)
    def _():
        drain(slot)
        if steps > 1:
            drain(1 - slot)


def weight_gradient(left, right, owners, place, relative, name, first=0, width=None):
    depth = left.shape[0] * left.shape[1]
    left, right = left.reshape(depth, -1), right.reshape(depth, -1)
    block, cols, width = 640, 1280, width or right.shape[1]
    if not relative:
        owners = left.shape[1] // block
    rows = left.shape[1] // owners
    steps = (left.shape[1] // block) * (width // cols)
    if relative:
        shapes = [sds(owners // 2, rows, width), sds(owners // 4, rows, width), sds(owners // 4, rows, width)]
    else:
        shapes = [sds(owners, rows, width)]

    def kernel(*refs):
        gradient_kernel(rows, steps, relative, len(shapes), *refs)

    return pl.pallas_call(
        kernel,
        grid=(left.shape[1] // block, width // cols),
        in_specs=[
            pl.BlockSpec(memory_space=pltpu.SMEM),
            pl.BlockSpec((depth, block), lambda i, j: (0, i)),
            pl.BlockSpec((depth, cols), lambda i, j: (0, j + first // cols)),
        ],
        out_specs=[pl.BlockSpec(memory_space=pl.ANY)] * len(shapes),
        out_shape=shapes,
        scratch_shapes=[pltpu.VMEM((2, block, cols), BF), pltpu.SemaphoreType.DMA((2, block // rows))],
        compiler_params=pltpu.CompilerParams(vmem_limit_bytes=60 << 20),
        cost_estimate=cost(2.5 * depth * left.shape[1] * width, [left, right] + shapes),
        name=name,
    )(place, left, right)


SWAP = [(0, 1), (1, 0)]


def row(vector):
    return vector.reshape(1, -1).astype(F32)


def after(value, *others):
    return lax.optimization_barrier((value, others))[0]


def both_groups(shard):
    if lax.axis_size("dp") != 2:
        return lax.psum(shard, "dp").astype(F32)
    return shard.astype(F32) + lax.ppermute(shard, "dp", SWAP).astype(F32)


class Whole:
    def __init__(self, owners):
        self.owners, self.mine, self.relative = owners, jnp.zeros((2,), jnp.int32), False

    def gather_small(self, vector):
        return lax.all_gather(vector.reshape(1, -1), "fsdp", axis=0, tiled=True)

    def gather(self, w):
        return lax.all_gather(w, "fsdp", axis=0, tiled=True)

    def first_stage(self, parts, *before):
        return parts

    def second_stage(self, parts, *before):
        return parts

    def joined(self, parts):
        return (jnp.concatenate([p[0] for p in parts], 2),)

    def third_stage(self, parts):
        whole = parts[0].reshape(-1, parts[0].shape[2])
        return lax.psum_scatter(whole, "fsdp", scatter_dimension=0, tiled=True)

    def scatter_small(self, shares):
        return lax.psum(lax.psum_scatter(shares, "fsdp", scatter_dimension=0, tiled=True)[0], "dp")


class Split:
    relative = True

    def __init__(self, owners):
        self.owners, self.count = owners, owners // 4
        self.mine = jnp.stack([lax.axis_index("x"), lax.axis_index("core")]).astype(jnp.int32)
        self.z = jnp.arange(self.count, dtype=jnp.int32)

    def gather(self, w):
        return lax.all_gather(w, ("z", "x", "core"), axis=0, tiled=True)

    def gather_small(self, vector):
        rows = vector.reshape(1, -1)

        def double(rows, axis, step, other):
            got = lax.ppermute(rows, axis, other)
            low = lax.rem(lax.axis_index(axis) // step, 2) == 0
            return jnp.concatenate([jnp.where(low, rows, got), jnp.where(low, got, rows)], 0)
        rows = double(rows, "core", 1, SWAP)
        rows = double(rows, "x", 1, SWAP)
        step = 1
        while step < self.count:
            rows = double(rows, "z", step, [(i, i ^ step) for i in range(self.count)])
            step *= 2
        return rows

    def first_stage(self, parts, *before):
        send, keep, pass_on = parts
        half = send.shape[0] // 2
        got = lax.ppermute(send, "core", SWAP)
        return after(pass_on, *before) + got[half:], keep, got

    def second_stage(self, parts, *before):
        passed, keep, got = parts
        half, keep = got.shape[0] // 2, after(keep, *before)
        got_x = lax.ppermute(passed, "x", SWAP)
        return (keep.astype(F32) + got[:half].astype(F32) + got_x.astype(F32)).astype(BF)

    def joined(self, parts):
        return tuple(jnp.concatenate(a, 2) for a in zip(*parts))

    def third_stage(self, total):
        return lax.psum_scatter(total, "z", scatter_dimension=0, tiled=True)[0]

    def scatter_small(self, shares):
        shares = shares.reshape(self.count, 2, 2, -1)

        def halve(rows, axis, here):
            kept = lax.dynamic_index_in_dim(rows, here, axis, keepdims=False)
            return kept, lax.dynamic_index_in_dim(rows, 1 - here, axis, keepdims=False)
        kept, sent = halve(shares, 2, self.mine[1])
        shares = kept + lax.ppermute(sent, "core", SWAP)
        kept, sent = halve(shares, 1, self.mine[0])
        shares = kept + lax.ppermute(sent, "x", SWAP)
        step = self.count // 2
        while step:
            shares = shares.reshape(2, step, -1)
            kept, sent = halve(shares, 0, lax.rem(lax.axis_index("z") // step, 2))
            shares = kept + lax.ppermute(sent, "z", [(i, i ^ step) for i in range(self.count)])
            step //= 2
        shares = shares.reshape(-1)
        if lax.axis_size("dp") != 2:
            return lax.psum(shares, "dp")
        return shares + lax.ppermute(shares, "dp", SWAP)


def row(vector):
    return vector.reshape(1, -1).astype(F32)


def layer(links, images, cotangent, w_qkv, w_out, w_up, w_down, *vectors):
    n, owners = images.shape[0], links.owners

    sizes = [v.shape[0] for v in vectors]
    small = links.gather_small(jnp.concatenate(vectors))
    full, first = [], 0
    for size in sizes:
        full.append(row(small[:, first:first + size]))
        first += size
    b_qv, b_out, b_up, b_down, gain_one, shift_one, gain_two, shift_two = full

    def image(a):
        return (a, "image")

    def rows(*shape, dtype=BF):
        return (sds(n, *shape, dtype=dtype), "image")

    def sums(width):
        return total(sds(8, width, dtype=F32))

    def gradient(left, right, name, first=0, width=None):
        return weight_gradient(left, right, owners, links.mine, links.relative, name, first, width)

    def by_columns(kernel, weight, rows_in, others, outs, name, flops, sum_width=0):
        def cut(a):
            if len(a.shape) == 2:
                return a, pl.BlockSpec((a.shape[0], D), lambda j, i: (0, j))
            return a, pl.BlockSpec((4, SP, D), lambda j, i: (i, 0, j))
        results = [cut(a) for a in outs]
        return grid_call(
            kernel, (outs[0].shape[2] // D, n // 4),
            [weight, (rows_in, pl.BlockSpec((4, SP, D), lambda j, i: (i, 0, 0)))] + [cut(a) for a in others],
            results, name, flops * n * SP)

    full_qkv = links.gather(w_qkv)
    normed_one, xpad, cpad, s_down = call(
        prepare_kernel, n, [image(images), image(cotangent), whole(gain_one), whole(shift_one)],
        [rows(SP, D), rows(SP, D), rows(SP, D), sums(D)], "prepare", 8 * n * SP * D * 50)
    middle = links.gather(after(jnp.concatenate([w_up, w_out], 1), normed_one))
    full_out = middle, pl.BlockSpec((D, D), lambda *at: (0, FF // D), pipeline_mode=pl.Buffered(1))
    bias = jnp.concatenate([b_qv[:, :D], jnp.zeros((1, D), F32), b_qv[:, D:]], 1)
    packed, = by_columns(
        qkv_kernel, (full_qkv, pl.BlockSpec((D, D), lambda j, i: (0, j))), normed_one, [bias], [sds(n, SP, 3 * D)],
        "qkv", 2.5 * D * 3 * D)
    full_down = links.gather(after(w_down, packed))
    mixed, logsum = call(
        attention_kernel, n, [image(packed)], [rows(SP, D), rows(H, SP, dtype=F32)], "attention", 1e5 * n * SP * H)
    hidden, normed_two = call(
        out_kernel, n,
        [full_out, image(xpad), image(mixed), whole(b_out), whole(gain_two), whole(shift_two)],
        [rows(SP, D, dtype=F32), rows(SP, D)], "out", 3 * D * D * n * SP)
    active, slope = by_columns(
        up_kernel, (middle, pl.BlockSpec((D, D), lambda j, i: (0, j))), normed_two, [b_up], [sds(n, SP, FF)] * 2,
        "up", 4 * D * FF)

    p_down = gradient(active, cpad, "g_down")
    staging = [pltpu.VMEM((D // 128, SEQ * n, 128), F32), pltpu.SemaphoreType.DMA((D // 128,))]
    result, = call(
        down_kernel, n, [whole(full_down), image(after(active, p_down)), image(hidden), whole(b_down)],
        [untouched(sds(SEQ * n, D, dtype=F32))], "down", 2.5 * D * FF * n * SP, staging)
    p_down = links.first_stage(p_down, result)
    d_inner, s_up = by_columns(
        down_back_kernel, (full_down, pl.BlockSpec((D, D), lambda j, i: (j, 0))), after(cpad, result, p_down[0]), [slope],
        [sds(n, SP, FF), sds(8, FF, dtype=F32)], "down_back", 3 * D * FF)
    p_up = gradient(normed_two, d_inner, "g_up_low", 0, FF // 2)
    p_up2 = gradient(normed_two, after(d_inner, p_up), "g_up_high", FF // 2, FF // 2)
    p_up = links.first_stage(p_up, p_up2)
    p_down = links.second_stage(p_down, p_up2)

    def pair(a):
        return a, pl.BlockSpec((2,) + tuple(a.shape[1:]), lambda i, k: (i, 0, 0))
    d_hidden, d_hidden_b, d_mixed, s_gain_two, s_shift_two, s_out = grid_call(
        up_back_kernel, (n // 2, 2),
        [(middle, pl.BlockSpec((D, FF // 2), lambda i, k: (0, k))),
         (after(d_inner, p_up2, p_up[0], p_down), pl.BlockSpec((2, SP, FF // 2), lambda i, k: (i, 0, k))),
         full_out, pair(hidden), pair(cpad), whole(gain_two)],
        [pair(sds(n, SP, D, dtype=F32)), pair(sds(n, SP, D)), pair(sds(n, SP, D)), sums(D), sums(D), sums(D)],
        "up_back", 3 * D * (D + FF) * n * SP, [pltpu.VMEM((2 * SP, D), F32)])
    p_down = links.third_stage(p_down)
    p_up = links.second_stage(p_up, d_hidden_b)
    p_out = gradient(mixed, after(d_hidden_b, p_up, p_down), "g_out")
    p_up = links.third_stage(p_up)
    p_up2 = links.first_stage(p_up2, p_out)
    p_out = links.first_stage(p_out)
    rest = links.joined([p_up2, p_out])
    d_packed, s_qv = call(
        attention_back_kernel, n, [image(packed), image(mixed), image(after(d_mixed, rest[0])), image(logsum)],
        [rows(SP, 3 * D), sums(2 * D)], "attention_back", 1.4e5 * n * SP * H)
    g_down = both_groups(after(p_down, d_packed))
    rest = links.second_stage(rest, d_packed)
    last = gradient(normed_one, after(d_packed, rest, p_up), "g_qkv")
    rest = links.third_stage(rest)
    last = links.first_stage(last)
    d_images, s_gain_one, s_shift_one = call(
        qkv_back_kernel, n,
        [whole(full_qkv), image(after(d_packed, last[0])), image(xpad), image(d_hidden), whole(gain_one)],
        [untouched(sds(SEQ * n, D, dtype=F32)), sums(D), sums(D)], "qkv_back", 3 * D * 3 * D * n * SP, staging)
    g_up = both_groups(after(p_up, last[0]))
    last = links.second_stage(last, d_images, rest)
    rest, s_gain_one = after((rest, s_gain_one), last)
    rest, g_qkv = both_groups(rest), both_groups(links.third_stage(last))
    g_up2, g_out = rest[:, :FF // 2], rest[:, FF // 2:]
    result, d_images = [jnp.transpose(a.reshape(SEQ, n, D), (1, 0, 2)) for a in (result, d_images)]
    g_up = jnp.concatenate([g_up, g_up2], 1)

    parts = [s_qv, s_out, s_up, s_down, s_gain_one, s_shift_one, s_gain_two, s_shift_two]
    share = links.scatter_small(jnp.concatenate([jnp.sum(s, 0).reshape(owners, -1) for s in parts], 1))
    small_grads, first = [], 0
    for size in sizes:
        small_grads.append(share[first:first + size])
        first += size
    return (result, d_images, g_qkv, g_out, g_up, g_down, *small_grads)


def solution(mesh):
    dp, owners = mesh.shape["dp"], mesh.shape["fsdp"]
    kind, fsdp = Whole, ("fsdp",)
    if dp == 2 and owners % 4 == 0 and (D // owners) % 16 == 0:
        kind, fsdp = Split, ("z", "x", "core")
        mesh = Mesh(mesh.devices.reshape(dp, owners // 4, 2, 2), ("dp",) + fsdp)
    images, matrix, vector = P(("dp",) + fsdp, None, None), P(fsdp, None), P(fsdp)
    specs = (images,) * 2 + (matrix,) * 4 + (vector,) * 8

    def run(*args):
        return layer(kind(owners), *args)

    return jax.shard_map(run, mesh=mesh, in_specs=specs, out_specs=specs, check_vma=False)
```

```python
import math

import jax
import jax.numpy as jnp
from jax import lax
from jax.experimental import pallas as pl
from jax.experimental.pallas import tpu as pltpu
from jax.sharding import Mesh
from jax.sharding import PartitionSpec as P

D = 1280
H = 16
HD = 80
FF = 5120
SEQ = 257
SP = 264
GROUP = 8
GW = GROUP * HD
EPS = 1e-06
SCALE = HD ** (-0.5)
NT = (((1,), (1,)), ((), ()))
BF = jnp.bfloat16
F32 = jnp.float32


def dot_nt(left, right):
    return lax.dot_general(left, right, NT, preferred_element_type=F32)


def dot_nn(left, right):
    return jnp.dot(left, right, preferred_element_type=F32)


def pad_rows(rows):
    return jnp.concatenate([rows, jnp.zeros((SP - SEQ, rows.shape[1]), rows.dtype)], 0)


def fold_rows(rows):
    return jnp.sum(rows.reshape(rows.shape[0] // 8, 8, rows.shape[1]), 0)


def standardize(rows):
    centered = rows - jnp.mean(rows, -1, keepdims=True)
    inverse = lax.rsqrt(jnp.mean(centered * centered, -1, keepdims=True) + EPS)
    return centered * inverse, inverse


def norm_gradient(e, xhat, inverse, gain):
    scaled = e * gain
    first = jnp.mean(scaled, -1, keepdims=True)
    second = jnp.mean(scaled * xhat, -1, keepdims=True)
    return inverse * (scaled - first - xhat * second)


def cost(flops, arrays):
    moved = sum(math.prod(a.shape) * a.dtype.itemsize for a in arrays)
    return pl.CostEstimate(flops=int(flops), transcendentals=0, bytes_accessed=moved)


def grid_call(kernel, grid, ins, outs, name, flops=0, scratch=()):
    return pl.pallas_call(
        kernel,
        grid=grid,
        in_specs=[spec for _, spec in ins],
        out_specs=[spec for _, spec in outs],
        out_shape=[a for a, _ in outs],
        scratch_shapes=list(scratch),
        compiler_params=pltpu.CompilerParams(vmem_limit_bytes=62 << 20),
        cost_estimate=cost(flops, [a for a, _ in ins] + [a for a, _ in outs]),
        name=name,
    )(*[a for a, _ in ins])


def whole(a):
    return a, pl.BlockSpec(tuple(a.shape), lambda *at: (0,) * len(a.shape), pipeline_mode=pl.Buffered(1))


def total(a):
    return a, pl.BlockSpec(tuple(a.shape), lambda *at: (0,) * len(a.shape))


def untouched(a):
    return a, pl.BlockSpec(memory_space=pl.ANY)


def call(kernel, n, ins, outs, name, flops=0, scratch=()):
    def specs(pairs):
        for a, kind in pairs:
            if kind == "image":
                kind = pl.BlockSpec((1,) + tuple(a.shape[1:]), lambda i, last=len(a.shape) - 1: (i,) + (0,) * last)
            yield a, kind
    return grid_call(kernel, (n,), list(specs(ins)), list(specs(outs)), name, flops, scratch)


def accumulate(ref, value):
    @pl.when(pl.program_id(0) == 0)
    def _():
        ref[...] = jnp.zeros_like(ref)
    ref[...] += value


def prepare_kernel(x_ref, c_ref, gain_ref, shift_ref, normed_ref, xpad_ref, cpad_ref, sum_ref):
    x = x_ref[0].astype(F32)
    xhat, _ = standardize(x)
    normed = xhat * gain_ref[...] + shift_ref[...]
    normed_ref[0] = pad_rows(normed).astype(BF)
    xpad_ref[0] = pad_rows(x).astype(BF)
    c = pad_rows(c_ref[0].astype(F32))
    cpad_ref[0] = c.astype(BF)
    accumulate(sum_ref, fold_rows(c))


def flat(ref):
    return ref[...].reshape(ref.shape[0] * ref.shape[1], ref.shape[2])


def qkv_kernel(w_ref, normed_ref, bias_ref, packed_ref):
    out = dot_nn(flat(normed_ref), w_ref[...]) + bias_ref[...]
    packed_ref[...] = out.astype(BF).reshape(packed_ref.shape)


def drop_tail(rows):
    tail = rows[SP - 8:]
    keep = lax.broadcasted_iota(jnp.int32, tail.shape, 0) < SEQ - (SP - 8)
    return jnp.concatenate([rows[:SP - 8], jnp.where(keep, tail, 0.0)], 0)


def attention_kernel(packed_ref, mixed_ref, lse_ref):
    def group(g, carry):
        base = g * GW
        here = pl.ds(pl.multiple_of(base, 128), GW)
        queries, keys, values = [
            packed_ref[0, :, pl.ds(pl.multiple_of(part * D + base, 128), GW)] for part in range(3)]
        values_t = values.astype(F32).T.astype(BF)
        outs, lses = [], []
        for j in range(GROUP):
            head = slice(j * HD, (j + 1) * HD)
            s = dot_nt(keys[:, head], queries[:, head])
            tail = s[SP - 8:]
            keep = lax.broadcasted_iota(jnp.int32, tail.shape, 0) < SEQ - (SP - 8)
            s = jnp.concatenate([s[:SP - 8], jnp.where(keep, tail, -1e30)], 0) * SCALE
            top = jnp.max(s, 0, keepdims=True)
            e = jnp.exp(s - top)
            total = jnp.sum(e, 0, keepdims=True)
            o = dot_nn(values_t[head], e.astype(BF)) * (1.0 / total)
            outs.append(o)
            lses.append(top + jnp.log(total))
        mixed_ref[0, :, pl.ds(pl.multiple_of(base, 128), GW)] = jnp.concatenate(outs, 0).T.astype(BF)
        lse_ref[0, pl.ds(pl.multiple_of(g * GROUP, 8), GROUP), :] = jnp.concatenate(lses, 0)
        return carry
    lax.fori_loop(0, H // GROUP, group, 0)


def out_kernel(w_ref, x_ref, mixed_ref, bias_ref, gain_ref, shift_ref, hidden_ref, normed_ref):
    hidden = flat(x_ref).astype(F32) + dot_nn(flat(mixed_ref), w_ref[...]) + bias_ref[...]
    hidden_ref[...] = hidden.reshape(hidden_ref.shape)
    xhat, _ = standardize(hidden)
    normed = xhat * gain_ref[...] + shift_ref[...]
    keep = lax.rem(lax.broadcasted_iota(jnp.int32, normed.shape, 0), SP) < SEQ
    normed_ref[...] = jnp.where(keep, normed, 0.0).astype(BF).reshape(normed_ref.shape)


def up_kernel(w_ref, normed_ref, bias_ref, active_ref, slope_ref):
    u = dot_nn(flat(normed_ref), w_ref[...]) + bias_ref[...]
    cdf = 0.5 * (1.0 + lax.erf(u * 0.7071067811865476))
    active_ref[...] = (u * cdf).astype(BF).reshape(active_ref.shape)
    slope_ref[...] = (cdf + u * jnp.exp(-0.5 * u * u) * 0.3989422804014327).astype(BF).reshape(slope_ref.shape)


def interleave(rows, out_ref, stage_ref, sems):
    image, last = pl.program_id(0), pl.num_programs(0) - 1
    tiles = stage_ref.shape[0]
    step = stage_ref.shape[1] // SEQ
    for k in range(tiles):
        stage_ref[k, pl.ds(image, SEQ, stride=step), :] = rows[:SEQ, k * 128:(k + 1) * 128]

    @pl.when(image == last)
    def _():
        copies = [pltpu.make_async_copy(stage_ref.at[k], out_ref.at[:, k * 128:(k + 1) * 128], sems.at[k]) for k in range(tiles)]
        for copy in copies:
            copy.start()
        for copy in copies:
            copy.wait()


def down_kernel(w_ref, active_ref, hidden_ref, bias_ref, result_ref, stage_ref, sems):
    result = hidden_ref[0] + dot_nn(active_ref[0], w_ref[...]) + bias_ref[...]
    interleave(result, result_ref, stage_ref, sems)


def down_back_kernel(w_ref, c_ref, slope_ref, dinner_ref, sum_ref):
    d = dot_nt(flat(c_ref), w_ref[...]) * flat(slope_ref).astype(F32)
    dinner_ref[...] = d.astype(BF).reshape(dinner_ref.shape)

    @pl.when(pl.program_id(1) == 0)
    def _():
        sum_ref[...] = jnp.zeros_like(sum_ref)
    sum_ref[...] += fold_rows(d)


def up_back_kernel(w_up_ref, dinner_ref, w_out_ref, hidden_ref, c_ref, gain_ref,
                   dhidden_ref, dhidden_b_ref, dmixed_ref, sum_gain_ref, sum_shift_ref, sum_out_ref, acc_ref):
    i, k = pl.program_id(0), pl.program_id(1)

    @pl.when(k == 0)
    def _():
        acc_ref[...] = dot_nt(flat(dinner_ref), w_up_ref[...])

    @pl.when(k > 0)
    def _():
        acc_ref[...] += dot_nt(flat(dinner_ref), w_up_ref[...])

    @pl.when(jnp.logical_and(i == 0, k == 0))
    def _():
        for ref in (sum_gain_ref, sum_shift_ref, sum_out_ref):
            ref[...] = jnp.zeros_like(ref)

    @pl.when(k == pl.num_programs(1) - 1)
    def _():
        for image in range(dhidden_ref.shape[0]):
            e = acc_ref[image * SP:(image + 1) * SP]
            xhat, inverse = standardize(hidden_ref[image])
            dhidden = c_ref[image].astype(F32) + norm_gradient(e, xhat, inverse, gain_ref[...])
            dhidden_ref[image] = dhidden
            dhidden_b = dhidden.astype(BF)
            dhidden_b_ref[image] = dhidden_b
            dmixed_ref[image] = dot_nt(dhidden_b, w_out_ref[...]).astype(BF)
            sum_gain_ref[...] += fold_rows(e * xhat)
            sum_shift_ref[...] += fold_rows(e)
            sum_out_ref[...] += fold_rows(dhidden)


def attention_back_kernel(packed_ref, mixed_ref, dmixed_ref, lse_ref, dpacked_ref, sum_ref):
    full = SEQ - 1

    @pl.when(pl.program_id(0) == 0)
    def _():
        sum_ref[...] = jnp.zeros_like(sum_ref)

    def group(g, carry):
        base = g * GW
        queries, keys, values = [
            packed_ref[0, :, pl.ds(pl.multiple_of(part * D + base, 128), GW)] for part in range(3)]
        here = pl.ds(pl.multiple_of(base, 128), GW)
        grads = dmixed_ref[0, :, here]
        product = grads.astype(F32) * mixed_ref[0, :, here].astype(F32)
        product_t = product[:full].T
        keys_t = keys.astype(F32).T
        keys_tb = keys_t[:, :full].astype(BF)
        lse = lse_ref[0, pl.ds(pl.multiple_of(g * GROUP, 8), GROUP), :]
        dq, dk, dv = [], [], []
        for j in range(GROUP):
            head = slice(j * HD, (j + 1) * HD)
            q, k, v, dm = queries[:full, head], keys[:, head], values[:, head], grads[:full, head]
            delta = jnp.sum(product_t[head], 0, keepdims=True)
            p = drop_tail(jnp.exp(dot_nt(k, q) * SCALE - lse[j:j + 1, :full]))
            dv.append(dot_nn(p.astype(BF), dm))
            ds = (p * (dot_nt(v, dm) - delta) * SCALE).astype(BF)
            dk.append(dot_nn(ds, q))
            dq.append(dot_nn(keys_tb[head], ds[:full])
                      + keys_t[head, full:full + 1] * ds[full:].astype(F32)[:1])
        dq = jnp.concatenate(dq, 0).T
        dk = jnp.concatenate(dk, 1)
        dv = jnp.concatenate(dv, 1)

        head_row = lax.broadcasted_iota(jnp.int32, (GROUP, GW), 0)
        lane = lax.broadcasted_iota(jnp.int32, (GROUP, GW), 1)
        mine = jnp.logical_and(lane >= head_row * HD, lane < (head_row + 1) * HD)
        diagonal = lax.broadcasted_iota(jnp.int32, (GROUP, GROUP), 0) == lax.broadcasted_iota(jnp.int32, (GROUP, GROUP), 1)

        def spread(rows):
            return jnp.where(mine, rows[full:].astype(F32)[:1], 0.0)

        def as_row(column):
            return jnp.sum(jnp.where(diagonal, column, 0.0), 0, keepdims=True)
        q, dm = spread(queries).astype(BF), spread(grads).astype(BF)
        delta = as_row(jnp.sum(spread(product), 1, keepdims=True))
        p = drop_tail(jnp.exp(dot_nt(keys, q) * SCALE - as_row(lse[:, full:full + 1])))
        ds = p * (dot_nt(values, dm) - delta) * SCALE
        dv = dv + dot_nn(p.astype(BF), dm)
        dk = dk + dot_nn(ds.astype(BF), q)
        ds_t = jnp.concatenate([ds, jnp.zeros((SP, 128 - GROUP), F32)], 1).T[:GROUP].astype(BF)
        dq_last = jnp.sum(jnp.where(mine, dot_nn(ds_t, keys), 0.0), 0, keepdims=True)
        tail = lax.broadcasted_iota(jnp.int32, (SP - full, GW), 0) == 0
        dq_last = jnp.where(tail, dq_last, 0.0)

        def out(part):
            return pl.ds(pl.multiple_of(part * D + base, 128), GW)
        dpacked_ref[0, :full, out(0)] = dq.astype(BF)
        dpacked_ref[0, full:, out(0)] = dq_last.astype(BF)
        dpacked_ref[0, :, out(1)] = dk.astype(BF)
        dpacked_ref[0, :, out(2)] = dv.astype(BF)
        sum_ref[:, out(0)] += fold_rows(dq) + dq_last
        sum_ref[:, out(1)] += fold_rows(dv)
        return carry
    lax.fori_loop(0, H // GROUP, group, 0)


def qkv_back_kernel(w_ref, dpacked_ref, x_ref, dhidden_ref, gain_ref,
                    dimages_ref, sum_gain_ref, sum_shift_ref, stage_ref, sems):
    e = dot_nt(dpacked_ref[0], w_ref[...])
    xhat, inverse = standardize(x_ref[0].astype(F32))
    dimages = dhidden_ref[0] + norm_gradient(e, xhat, inverse, gain_ref[...])
    interleave(dimages, dimages_ref, stage_ref, sems)
    accumulate(sum_gain_ref, fold_rows(e * xhat))
    accumulate(sum_shift_ref, fold_rows(e))


def sds(*shape, dtype=BF):
    return jax.ShapeDtypeStruct(shape, dtype)


def gradient_kernel(rows, steps, relative, spots, place_ref, l_ref, r_ref, *rest):
    outs, stage, sems = rest[:spots], rest[spots], rest[spots + 1]
    i, j = pl.program_id(0), pl.program_id(1)
    step = i * pl.num_programs(1) + j
    block, width = stage.shape[1], stage.shape[2]
    per = block // rows

    def copy(slot, t, out, at, cols):
        return pltpu.make_async_copy(stage.at[slot, t * rows:(t + 1) * rows, :], out.at[at, :, cols], sems.at[slot, t])

    def drain(slot):
        for t in range(per):
            copy(slot, t, outs[0], 0, pl.ds(0, width)).wait()

    slot = lax.rem(step, 2)

    @pl.when(step >= 2)
    def _():
        drain(slot)
    stage[slot] = lax.dot_general(l_ref[...], r_ref[...], (((0,), (0,)), ((), ())), preferred_element_type=F32).astype(BF)
    cols = pl.ds(pl.multiple_of(j * width, 128), width)
    for t in range(per):
        owner = i * per + t
        if not relative:
            copy(slot, t, outs[0], owner, cols).start()
            continue
        core = lax.rem(owner, 2) ^ place_ref[1]
        x = lax.rem(owner // 2, 2) ^ place_ref[0]
        z = owner // 4

        @pl.when(core == 1)
        def _():
            copy(slot, t, outs[0], x * (outs[0].shape[0] // 2) + z, cols).start()

        @pl.when(jnp.logical_and(core == 0, x == 0))
        def _():
            copy(slot, t, outs[1], z, cols).start()

        @pl.when(jnp.logical_and(core == 0, x == 1))
        def _():
            copy(slot, t, outs[2], z, cols).start()

    @pl.when(step == steps - 1)
    def _():
        drain(slot)
        if steps > 1:
            drain(1 - slot)


def weight_gradient(left, right, owners, place, relative, name, first=0, width=None):
    depth = left.shape[0] * left.shape[1]
    left, right = left.reshape(depth, -1), right.reshape(depth, -1)
    block, cols, width = 640, 1280, width or right.shape[1]
    if not relative:
        owners = left.shape[1] // block
    rows = left.shape[1] // owners
    steps = (left.shape[1] // block) * (width // cols)
    if relative:
        shapes = [sds(owners // 2, rows, width), sds(owners // 4, rows, width), sds(owners // 4, rows, width)]
    else:
        shapes = [sds(owners, rows, width)]

    def kernel(*refs):
        gradient_kernel(rows, steps, relative, len(shapes), *refs)

    return pl.pallas_call(
        kernel,
        grid=(left.shape[1] // block, width // cols),
        in_specs=[
            pl.BlockSpec(memory_space=pltpu.SMEM),
            pl.BlockSpec((depth, block), lambda i, j: (0, i)),
            pl.BlockSpec((depth, cols), lambda i, j: (0, j + first // cols)),
        ],
        out_specs=[pl.BlockSpec(memory_space=pl.ANY)] * len(shapes),
        out_shape=shapes,
        scratch_shapes=[pltpu.VMEM((2, block, cols), BF), pltpu.SemaphoreType.DMA((2, block // rows))],
        compiler_params=pltpu.CompilerParams(vmem_limit_bytes=60 << 20),
        cost_estimate=cost(2.5 * depth * left.shape[1] * width, [left, right] + shapes),
        name=name,
    )(place, left, right)


SWAP = [(0, 1), (1, 0)]


def row(vector):
    return vector.reshape(1, -1).astype(F32)


def after(value, *others):
    return lax.optimization_barrier((value, others))[0]


def both_groups(shard):
    if lax.axis_size("dp") != 2:
        return lax.psum(shard, "dp").astype(F32)
    return shard.astype(F32) + lax.ppermute(shard, "dp", SWAP).astype(F32)


class Whole:
    def __init__(self, owners):
        self.owners, self.mine, self.relative = owners, jnp.zeros((2,), jnp.int32), False

    def gather_small(self, vector):
        return lax.all_gather(vector.reshape(1, -1), "fsdp", axis=0, tiled=True)

    def gather(self, w):
        return lax.all_gather(w, "fsdp", axis=0, tiled=True)

    def first_stage(self, parts, *before):
        return parts

    def second_stage(self, parts, *before):
        return parts

    def joined(self, parts):
        return (jnp.concatenate([p[0] for p in parts], 2),)

    def third_stage(self, parts):
        whole = parts[0].reshape(-1, parts[0].shape[2])
        return lax.psum_scatter(whole, "fsdp", scatter_dimension=0, tiled=True)

    def scatter_small(self, shares):
        return lax.psum(lax.psum_scatter(shares, "fsdp", scatter_dimension=0, tiled=True)[0], "dp")


class Split:
    relative = True

    def __init__(self, owners):
        self.owners, self.count = owners, owners // 4
        self.mine = jnp.stack([lax.axis_index("x"), lax.axis_index("core")]).astype(jnp.int32)
        self.z = jnp.arange(self.count, dtype=jnp.int32)

    def gather(self, w):
        return lax.all_gather(w, ("z", "x", "core"), axis=0, tiled=True)

    def gather_small(self, vector):
        rows = vector.reshape(1, -1)

        def double(rows, axis, step, other):
            got = lax.ppermute(rows, axis, other)
            low = lax.rem(lax.axis_index(axis) // step, 2) == 0
            return jnp.concatenate([jnp.where(low, rows, got), jnp.where(low, got, rows)], 0)
        rows = double(rows, "core", 1, SWAP)
        rows = double(rows, "x", 1, SWAP)
        step = 1
        while step < self.count:
            rows = double(rows, "z", step, [(i, i ^ step) for i in range(self.count)])
            step *= 2
        return rows

    def first_stage(self, parts, *before):
        send, keep, pass_on = parts
        half = send.shape[0] // 2
        got = lax.ppermute(send, "core", SWAP)
        return after(pass_on, *before) + got[half:], keep, got

    def second_stage(self, parts, *before):
        passed, keep, got = parts
        half, keep = got.shape[0] // 2, after(keep, *before)
        got_x = lax.ppermute(passed, "x", SWAP)
        return (keep.astype(F32) + got[:half].astype(F32) + got_x.astype(F32)).astype(BF)

    def joined(self, parts):
        return tuple(jnp.concatenate(a, 2) for a in zip(*parts))

    def third_stage(self, total):
        return lax.psum_scatter(total, "z", scatter_dimension=0, tiled=True)[0]

    def scatter_small(self, shares):
        shares = shares.reshape(self.count, 2, 2, -1)

        def halve(rows, axis, here):
            kept = lax.dynamic_index_in_dim(rows, here, axis, keepdims=False)
            return kept, lax.dynamic_index_in_dim(rows, 1 - here, axis, keepdims=False)
        kept, sent = halve(shares, 2, self.mine[1])
        shares = kept + lax.ppermute(sent, "core", SWAP)
        kept, sent = halve(shares, 1, self.mine[0])
        shares = kept + lax.ppermute(sent, "x", SWAP)
        step = self.count // 2
        while step:
            shares = shares.reshape(2, step, -1)
            kept, sent = halve(shares, 0, lax.rem(lax.axis_index("z") // step, 2))
            shares = kept + lax.ppermute(sent, "z", [(i, i ^ step) for i in range(self.count)])
            step //= 2
        shares = shares.reshape(-1)
        if lax.axis_size("dp") != 2:
            return lax.psum(shares, "dp")
        return shares + lax.ppermute(shares, "dp", SWAP)


def row(vector):
    return vector.reshape(1, -1).astype(F32)


def layer(links, images, cotangent, w_qkv, w_out, w_up, w_down, *vectors):
    n, owners = images.shape[0], links.owners

    sizes = [v.shape[0] for v in vectors]
    small = links.gather_small(jnp.concatenate(vectors))
    full, first = [], 0
    for size in sizes:
        full.append(row(small[:, first:first + size]))
        first += size
    b_qv, b_out, b_up, b_down, gain_one, shift_one, gain_two, shift_two = full

    def image(a):
        return (a, "image")

    def rows(*shape, dtype=BF):
        return (sds(n, *shape, dtype=dtype), "image")

    def sums(width):
        return total(sds(8, width, dtype=F32))

    def gradient(left, right, name, first=0, width=None):
        return weight_gradient(left, right, owners, links.mine, links.relative, name, first, width)

    def by_columns(kernel, weight, rows_in, others, outs, name, flops, sum_width=0):
        def cut(a):
            if len(a.shape) == 2:
                return a, pl.BlockSpec((a.shape[0], D), lambda j, i: (0, j))
            return a, pl.BlockSpec((4, SP, D), lambda j, i: (i, 0, j))
        results = [cut(a) for a in outs]
        return grid_call(
            kernel, (outs[0].shape[2] // D, n // 4),
            [weight, (rows_in, pl.BlockSpec((4, SP, D), lambda j, i: (i, 0, 0)))] + [cut(a) for a in others],
            results, name, flops * n * SP)

    full_qkv = links.gather(w_qkv)
    normed_one, xpad, cpad, s_down = call(
        prepare_kernel, n, [image(images), image(cotangent), whole(gain_one), whole(shift_one)],
        [rows(SP, D), rows(SP, D), rows(SP, D), sums(D)], "prepare", 8 * n * SP * D * 50)
    middle = links.gather(after(jnp.concatenate([w_up, w_out], 1), normed_one))
    full_out = middle, pl.BlockSpec((D, D), lambda *at: (0, FF // D), pipeline_mode=pl.Buffered(1))
    bias = jnp.concatenate([b_qv[:, :D], jnp.zeros((1, D), F32), b_qv[:, D:]], 1)
    packed, = by_columns(
        qkv_kernel, (full_qkv, pl.BlockSpec((D, D), lambda j, i: (0, j))), normed_one, [bias], [sds(n, SP, 3 * D)],
        "qkv", 2.5 * D * 3 * D)
    full_down = links.gather(after(w_down, packed))
    mixed, logsum = call(
        attention_kernel, n, [image(packed)], [rows(SP, D), rows(H, SP, dtype=F32)], "attention", 1e5 * n * SP * H)
    hidden, normed_two = call(
        out_kernel, n,
        [full_out, image(xpad), image(mixed), whole(b_out), whole(gain_two), whole(shift_two)],
        [rows(SP, D, dtype=F32), rows(SP, D)], "out", 3 * D * D * n * SP)
    active, slope = by_columns(
        up_kernel, (middle, pl.BlockSpec((D, D), lambda j, i: (0, j))), normed_two, [b_up], [sds(n, SP, FF)] * 2,
        "up", 4 * D * FF)

    p_down = gradient(active, cpad, "g_down")
    d_inner, s_up = by_columns(
        down_back_kernel, (full_down, pl.BlockSpec((D, D), lambda j, i: (j, 0))), after(cpad, p_down), [slope],
        [sds(n, SP, FF), sds(8, FF, dtype=F32)], "down_back", 3 * D * FF)
    p_down = links.first_stage(p_down, d_inner)
    p_up = gradient(normed_two, after(d_inner, p_down[0]), "g_up_low", 0, FF // 2)
    p_up2 = gradient(normed_two, after(d_inner, p_up), "g_up_high", FF // 2, FF // 2)
    p_up = links.first_stage(p_up, p_up2)

    def pair(a):
        return a, pl.BlockSpec((2,) + tuple(a.shape[1:]), lambda i, k: (i, 0, 0))
    d_hidden, d_hidden_b, d_mixed, s_gain_two, s_shift_two, s_out = grid_call(
        up_back_kernel, (n // 2, 2),
        [(middle, pl.BlockSpec((D, FF // 2), lambda i, k: (0, k))),
         (after(d_inner, p_up2, p_up[0]), pl.BlockSpec((2, SP, FF // 2), lambda i, k: (i, 0, k))),
         full_out, pair(hidden), pair(cpad), whole(gain_two)],
        [pair(sds(n, SP, D, dtype=F32)), pair(sds(n, SP, D)), pair(sds(n, SP, D)), sums(D), sums(D), sums(D)],
        "up_back", 3 * D * (D + FF) * n * SP, [pltpu.VMEM((2 * SP, D), F32)])
    p_down = links.second_stage(p_down, d_hidden_b)
    p_up = links.second_stage(p_up, d_hidden_b)
    p_out = gradient(mixed, after(d_hidden_b, p_down, p_up), "g_out")
    p_down = links.third_stage(p_down)
    p_up2 = links.first_stage(p_up2, p_out)
    p_out = links.first_stage(p_out)
    rest = links.joined([p_up2, p_out])
    d_packed, s_qv = call(
        attention_back_kernel, n, [image(packed), image(mixed), image(after(d_mixed, rest[0])), image(logsum)],
        [rows(SP, 3 * D), sums(2 * D)], "attention_back", 1.4e5 * n * SP * H)
    rest = links.second_stage(rest, d_packed)
    p_up = links.third_stage(after(p_up, p_down, d_packed))
    last = gradient(normed_one, after(d_packed, rest, p_down), "g_qkv")
    last = links.first_stage(after(last, p_up))
    rest = links.third_stage(after(rest, p_up))
    staging = [pltpu.VMEM((D // 128, SEQ * n, 128), F32), pltpu.SemaphoreType.DMA((D // 128,))]
    d_images, s_gain_one, s_shift_one = call(
        qkv_back_kernel, n,
        [whole(full_qkv), image(after(d_packed, last[0])), image(xpad), image(d_hidden), whole(gain_one)],
        [untouched(sds(SEQ * n, D, dtype=F32)), sums(D), sums(D)], "qkv_back", 3 * D * 3 * D * n * SP, staging)
    g_down, g_up = both_groups(after(p_down, last[0])), both_groups(after(p_up, last[0]))
    last = links.second_stage(last, d_images, rest)
    result, = call(
        down_kernel, n, [whole(full_down), image(after(active, last)), image(hidden), whole(b_down)],
        [untouched(sds(SEQ * n, D, dtype=F32))], "down", 2.5 * D * FF * n * SP, staging)
    rest = both_groups(after(rest, last))
    last, rest, g_down, g_up, s_gain_one = after((links.third_stage(last), rest, g_down, g_up, s_gain_one), result)
    g_qkv = both_groups(last)
    g_up2, g_out = rest[:, :FF // 2], rest[:, FF // 2:]
    result, d_images = [jnp.transpose(a.reshape(SEQ, n, D), (1, 0, 2)) for a in (result, d_images)]
    g_up = jnp.concatenate([g_up, g_up2], 1)

    parts = [s_qv, s_out, s_up, s_down, s_gain_one, s_shift_one, s_gain_two, s_shift_two]
    share = links.scatter_small(jnp.concatenate([jnp.sum(s, 0).reshape(owners, -1) for s in parts], 1))
    small_grads, first = [], 0
    for size in sizes:
        small_grads.append(share[first:first + size])
        first += size
    return (result, d_images, g_qkv, g_out, g_up, g_down, *small_grads)


def solution(mesh):
    dp, owners = mesh.shape["dp"], mesh.shape["fsdp"]
    kind, fsdp = Whole, ("fsdp",)
    if dp == 2 and owners % 4 == 0 and (D // owners) % 16 == 0:
        kind, fsdp = Split, ("z", "x", "core")
        mesh = Mesh(mesh.devices.reshape(dp, owners // 4, 2, 2), ("dp",) + fsdp)
    images, matrix, vector = P(("dp",) + fsdp, None, None), P(fsdp, None), P(fsdp)
    specs = (images,) * 2 + (matrix,) * 4 + (vector,) * 8

    def run(*args):
        return layer(kind(owners), *args)

    return jax.shard_map(run, mesh=mesh, in_specs=specs, out_specs=specs, check_vma=False)
```

```python
import math

import jax
import jax.numpy as jnp
from jax import lax
from jax.experimental import pallas as pl
from jax.experimental.pallas import tpu as pltpu
from jax.sharding import Mesh
from jax.sharding import PartitionSpec as P

D = 1280
H = 16
HD = 80
FF = 5120
SEQ = 257
SP = 264
GROUP = 8
GW = GROUP * HD
EPS = 1e-06
SCALE = HD ** (-0.5)
NT = (((1,), (1,)), ((), ()))
BF = jnp.bfloat16
F32 = jnp.float32


def dot_nt(left, right):
    return lax.dot_general(left, right, NT, preferred_element_type=F32)


def dot_nn(left, right):
    return jnp.dot(left, right, preferred_element_type=F32)


def pad_rows(rows):
    return jnp.concatenate([rows, jnp.zeros((SP - SEQ, rows.shape[1]), rows.dtype)], 0)


def fold_rows(rows):
    return jnp.sum(rows.reshape(rows.shape[0] // 8, 8, rows.shape[1]), 0)


def standardize(rows):
    centered = rows - jnp.mean(rows, -1, keepdims=True)
    inverse = lax.rsqrt(jnp.mean(centered * centered, -1, keepdims=True) + EPS)
    return centered * inverse, inverse


def norm_gradient(e, xhat, inverse, gain):
    scaled = e * gain
    first = jnp.mean(scaled, -1, keepdims=True)
    second = jnp.mean(scaled * xhat, -1, keepdims=True)
    return inverse * (scaled - first - xhat * second)


def cost(flops, arrays):
    moved = sum(math.prod(a.shape) * a.dtype.itemsize for a in arrays)
    return pl.CostEstimate(flops=int(flops), transcendentals=0, bytes_accessed=moved)


def grid_call(kernel, grid, ins, outs, name, flops=0, scratch=()):
    return pl.pallas_call(
        kernel,
        grid=grid,
        in_specs=[spec for _, spec in ins],
        out_specs=[spec for _, spec in outs],
        out_shape=[a for a, _ in outs],
        scratch_shapes=list(scratch),
        compiler_params=pltpu.CompilerParams(vmem_limit_bytes=62 << 20),
        cost_estimate=cost(flops, [a for a, _ in ins] + [a for a, _ in outs]),
        name=name,
    )(*[a for a, _ in ins])


def whole(a):
    return a, pl.BlockSpec(tuple(a.shape), lambda *at: (0,) * len(a.shape), pipeline_mode=pl.Buffered(1))


def total(a):
    return a, pl.BlockSpec(tuple(a.shape), lambda *at: (0,) * len(a.shape))


def untouched(a):
    return a, pl.BlockSpec(memory_space=pl.ANY)


def call(kernel, n, ins, outs, name, flops=0, scratch=()):
    def specs(pairs):
        for a, kind in pairs:
            if kind == "image":
                kind = pl.BlockSpec((1,) + tuple(a.shape[1:]), lambda i, last=len(a.shape) - 1: (i,) + (0,) * last)
            yield a, kind
    return grid_call(kernel, (n,), list(specs(ins)), list(specs(outs)), name, flops, scratch)


def accumulate(ref, value):
    @pl.when(pl.program_id(0) == 0)
    def _():
        ref[...] = jnp.zeros_like(ref)
    ref[...] += value


def prepare_kernel(x_ref, c_ref, gain_ref, shift_ref, normed_ref, xpad_ref, cpad_ref, sum_ref):
    x = x_ref[0].astype(F32)
    xhat, _ = standardize(x)
    normed = xhat * gain_ref[...] + shift_ref[...]
    normed_ref[0] = pad_rows(normed).astype(BF)
    xpad_ref[0] = pad_rows(x).astype(BF)
    c = pad_rows(c_ref[0].astype(F32))
    cpad_ref[0] = c.astype(BF)
    accumulate(sum_ref, fold_rows(c))


def flat(ref):
    return ref[...].reshape(ref.shape[0] * ref.shape[1], ref.shape[2])


def qkv_kernel(w_ref, normed_ref, bias_ref, packed_ref):
    out = dot_nn(flat(normed_ref), w_ref[...]) + bias_ref[...]
    packed_ref[...] = out.astype(BF).reshape(packed_ref.shape)


def drop_tail(rows):
    tail = rows[SP - 8:]
    keep = lax.broadcasted_iota(jnp.int32, tail.shape, 0) < SEQ - (SP - 8)
    return jnp.concatenate([rows[:SP - 8], jnp.where(keep, tail, 0.0)], 0)


def attention_kernel(packed_ref, mixed_ref, lse_ref):
    def group(g, carry):
        base = g * GW
        here = pl.ds(pl.multiple_of(base, 128), GW)
        queries, keys, values = [
            packed_ref[0, :, pl.ds(pl.multiple_of(part * D + base, 128), GW)] for part in range(3)]
        values_t = values.astype(F32).T.astype(BF)
        outs, lses = [], []
        for j in range(GROUP):
            head = slice(j * HD, (j + 1) * HD)
            s = dot_nt(keys[:, head], queries[:, head])
            tail = s[SP - 8:]
            keep = lax.broadcasted_iota(jnp.int32, tail.shape, 0) < SEQ - (SP - 8)
            s = jnp.concatenate([s[:SP - 8], jnp.where(keep, tail, -1e30)], 0) * SCALE
            top = jnp.max(s, 0, keepdims=True)
            e = jnp.exp(s - top)
            total = jnp.sum(e, 0, keepdims=True)
            o = dot_nn(values_t[head], e.astype(BF)) * (1.0 / total)
            outs.append(o)
            lses.append(top + jnp.log(total))
        mixed_ref[0, :, pl.ds(pl.multiple_of(base, 128), GW)] = jnp.concatenate(outs, 0).T.astype(BF)
        lse_ref[0, pl.ds(pl.multiple_of(g * GROUP, 8), GROUP), :] = jnp.concatenate(lses, 0)
        return carry
    lax.fori_loop(0, H // GROUP, group, 0)


def out_kernel(w_ref, x_ref, mixed_ref, bias_ref, gain_ref, shift_ref, hidden_ref, normed_ref):
    hidden = flat(x_ref).astype(F32) + dot_nn(flat(mixed_ref), w_ref[...]) + bias_ref[...]
    hidden_ref[...] = hidden.reshape(hidden_ref.shape)
    xhat, _ = standardize(hidden)
    normed = xhat * gain_ref[...] + shift_ref[...]
    keep = lax.rem(lax.broadcasted_iota(jnp.int32, normed.shape, 0), SP) < SEQ
    normed_ref[...] = jnp.where(keep, normed, 0.0).astype(BF).reshape(normed_ref.shape)


def up_kernel(w_ref, normed_ref, bias_ref, active_ref, slope_ref):
    u = dot_nn(flat(normed_ref), w_ref[...]) + bias_ref[...]
    cdf = 0.5 * (1.0 + lax.erf(u * 0.7071067811865476))
    active_ref[...] = (u * cdf).astype(BF).reshape(active_ref.shape)
    slope_ref[...] = (cdf + u * jnp.exp(-0.5 * u * u) * 0.3989422804014327).astype(BF).reshape(slope_ref.shape)


def interleave(rows, out_ref, stage_ref, sems):
    image, last = pl.program_id(0), pl.num_programs(0) - 1
    tiles = stage_ref.shape[0]
    step = stage_ref.shape[1] // SEQ
    for k in range(tiles):
        stage_ref[k, pl.ds(image, SEQ, stride=step), :] = rows[:SEQ, k * 128:(k + 1) * 128]

    @pl.when(image == last)
    def _():
        copies = [pltpu.make_async_copy(stage_ref.at[k], out_ref.at[:, k * 128:(k + 1) * 128], sems.at[k]) for k in range(tiles)]
        for copy in copies:
            copy.start()
        for copy in copies:
            copy.wait()


def down_kernel(w_ref, active_ref, hidden_ref, bias_ref, result_ref, stage_ref, sems):
    result = hidden_ref[0] + dot_nn(active_ref[0], w_ref[...]) + bias_ref[...]
    interleave(result, result_ref, stage_ref, sems)


def down_back_kernel(w_ref, c_ref, slope_ref, dinner_ref, sum_ref):
    d = dot_nt(flat(c_ref), w_ref[...]) * flat(slope_ref).astype(F32)
    dinner_ref[...] = d.astype(BF).reshape(dinner_ref.shape)

    @pl.when(pl.program_id(1) == 0)
    def _():
        sum_ref[...] = jnp.zeros_like(sum_ref)
    sum_ref[...] += fold_rows(d)


def up_back_kernel(w_up_ref, dinner_ref, w_out_ref, hidden_ref, c_ref, gain_ref,
                   dhidden_ref, dhidden_b_ref, dmixed_ref, sum_gain_ref, sum_shift_ref, sum_out_ref, acc_ref):
    i, k = pl.program_id(0), pl.program_id(1)

    @pl.when(k == 0)
    def _():
        acc_ref[...] = dot_nt(flat(dinner_ref), w_up_ref[...])

    @pl.when(k > 0)
    def _():
        acc_ref[...] += dot_nt(flat(dinner_ref), w_up_ref[...])

    @pl.when(jnp.logical_and(i == 0, k == 0))
    def _():
        for ref in (sum_gain_ref, sum_shift_ref, sum_out_ref):
            ref[...] = jnp.zeros_like(ref)

    @pl.when(k == pl.num_programs(1) - 1)
    def _():
        for image in range(dhidden_ref.shape[0]):
            e = acc_ref[image * SP:(image + 1) * SP]
            xhat, inverse = standardize(hidden_ref[image])
            dhidden = c_ref[image].astype(F32) + norm_gradient(e, xhat, inverse, gain_ref[...])
            dhidden_ref[image] = dhidden
            dhidden_b = dhidden.astype(BF)
            dhidden_b_ref[image] = dhidden_b
            dmixed_ref[image] = dot_nt(dhidden_b, w_out_ref[...]).astype(BF)
            sum_gain_ref[...] += fold_rows(e * xhat)
            sum_shift_ref[...] += fold_rows(e)
            sum_out_ref[...] += fold_rows(dhidden)


def attention_back_kernel(packed_ref, mixed_ref, dmixed_ref, lse_ref, dpacked_ref, sum_ref):
    full = SEQ - 1

    @pl.when(pl.program_id(0) == 0)
    def _():
        sum_ref[...] = jnp.zeros_like(sum_ref)

    def group(g, carry):
        base = g * GW
        queries, keys, values = [
            packed_ref[0, :, pl.ds(pl.multiple_of(part * D + base, 128), GW)] for part in range(3)]
        here = pl.ds(pl.multiple_of(base, 128), GW)
        grads = dmixed_ref[0, :, here]
        product = grads.astype(F32) * mixed_ref[0, :, here].astype(F32)
        product_t = product[:full].T
        keys_t = keys.astype(F32).T
        keys_tb = keys_t[:, :full].astype(BF)
        lse = lse_ref[0, pl.ds(pl.multiple_of(g * GROUP, 8), GROUP), :]
        dq, dk, dv = [], [], []
        for j in range(GROUP):
            head = slice(j * HD, (j + 1) * HD)
            q, k, v, dm = queries[:full, head], keys[:, head], values[:, head], grads[:full, head]
            delta = jnp.sum(product_t[head], 0, keepdims=True)
            p = drop_tail(jnp.exp(dot_nt(k, q) * SCALE - lse[j:j + 1, :full]))
            dv.append(dot_nn(p.astype(BF), dm))
            ds = (p * (dot_nt(v, dm) - delta) * SCALE).astype(BF)
            dk.append(dot_nn(ds, q))
            dq.append(dot_nn(keys_tb[head], ds[:full])
                      + keys_t[head, full:full + 1] * ds[full:].astype(F32)[:1])
        dq = jnp.concatenate(dq, 0).T
        dk = jnp.concatenate(dk, 1)
        dv = jnp.concatenate(dv, 1)

        head_row = lax.broadcasted_iota(jnp.int32, (GROUP, GW), 0)
        lane = lax.broadcasted_iota(jnp.int32, (GROUP, GW), 1)
        mine = jnp.logical_and(lane >= head_row * HD, lane < (head_row + 1) * HD)
        diagonal = lax.broadcasted_iota(jnp.int32, (GROUP, GROUP), 0) == lax.broadcasted_iota(jnp.int32, (GROUP, GROUP), 1)

        def spread(rows):
            return jnp.where(mine, rows[full:].astype(F32)[:1], 0.0)

        def as_row(column):
            return jnp.sum(jnp.where(diagonal, column, 0.0), 0, keepdims=True)
        q, dm = spread(queries).astype(BF), spread(grads).astype(BF)
        delta = as_row(jnp.sum(spread(product), 1, keepdims=True))
        p = drop_tail(jnp.exp(dot_nt(keys, q) * SCALE - as_row(lse[:, full:full + 1])))
        ds = p * (dot_nt(values, dm) - delta) * SCALE
        dv = dv + dot_nn(p.astype(BF), dm)
        dk = dk + dot_nn(ds.astype(BF), q)
        ds_t = jnp.concatenate([ds, jnp.zeros((SP, 128 - GROUP), F32)], 1).T[:GROUP].astype(BF)
        dq_last = jnp.sum(jnp.where(mine, dot_nn(ds_t, keys), 0.0), 0, keepdims=True)
        tail = lax.broadcasted_iota(jnp.int32, (SP - full, GW), 0) == 0
        dq_last = jnp.where(tail, dq_last, 0.0)

        def out(part):
            return pl.ds(pl.multiple_of(part * D + base, 128), GW)
        dpacked_ref[0, :full, out(0)] = dq.astype(BF)
        dpacked_ref[0, full:, out(0)] = dq_last.astype(BF)
        dpacked_ref[0, :, out(1)] = dk.astype(BF)
        dpacked_ref[0, :, out(2)] = dv.astype(BF)
        sum_ref[:, out(0)] += fold_rows(dq) + dq_last
        sum_ref[:, out(1)] += fold_rows(dv)
        return carry
    lax.fori_loop(0, H // GROUP, group, 0)


def qkv_back_kernel(w_ref, dpacked_ref, x_ref, dhidden_ref, gain_ref,
                    dimages_ref, sum_gain_ref, sum_shift_ref, stage_ref, sems):
    e = dot_nt(dpacked_ref[0], w_ref[...])
    xhat, inverse = standardize(x_ref[0].astype(F32))
    dimages = dhidden_ref[0] + norm_gradient(e, xhat, inverse, gain_ref[...])
    interleave(dimages, dimages_ref, stage_ref, sems)
    accumulate(sum_gain_ref, fold_rows(e * xhat))
    accumulate(sum_shift_ref, fold_rows(e))


def sds(*shape, dtype=BF):
    return jax.ShapeDtypeStruct(shape, dtype)


def gradient_kernel(rows, steps, relative, spots, place_ref, l_ref, r_ref, *rest):
    outs, stage, sems = rest[:spots], rest[spots], rest[spots + 1]
    i, j = pl.program_id(0), pl.program_id(1)
    step = i * pl.num_programs(1) + j
    block, width = stage.shape[1], stage.shape[2]
    per = block // rows

    def copy(slot, t, out, at, cols):
        return pltpu.make_async_copy(stage.at[slot, t * rows:(t + 1) * rows, :], out.at[at, :, cols], sems.at[slot, t])

    def drain(slot):
        for t in range(per):
            copy(slot, t, outs[0], 0, pl.ds(0, width)).wait()

    slot = lax.rem(step, 2)

    @pl.when(step >= 2)
    def _():
        drain(slot)
    stage[slot] = lax.dot_general(l_ref[...], r_ref[...], (((0,), (0,)), ((), ())), preferred_element_type=F32).astype(BF)
    cols = pl.ds(pl.multiple_of(j * width, 128), width)
    for t in range(per):
        owner = i * per + t
        if not relative:
            copy(slot, t, outs[0], owner, cols).start()
            continue
        core = lax.rem(owner, 2) ^ place_ref[1]
        x = lax.rem(owner // 2, 2) ^ place_ref[0]
        z = owner // 4

        @pl.when(core == 1)
        def _():
            copy(slot, t, outs[0], x * (outs[0].shape[0] // 2) + z, cols).start()

        @pl.when(jnp.logical_and(core == 0, x == 0))
        def _():
            copy(slot, t, outs[1], z, cols).start()

        @pl.when(jnp.logical_and(core == 0, x == 1))
        def _():
            copy(slot, t, outs[2], z, cols).start()

    @pl.when(step == steps - 1)
    def _():
        drain(slot)
        if steps > 1:
            drain(1 - slot)


def weight_gradient(left, right, owners, place, relative, name, first=0, width=None):
    depth = left.shape[0] * left.shape[1]
    left, right = left.reshape(depth, -1), right.reshape(depth, -1)
    block, cols, width = 640, 1280, width or right.shape[1]
    if not relative:
        owners = left.shape[1] // block
    rows = left.shape[1] // owners
    steps = (left.shape[1] // block) * (width // cols)
    if relative:
        shapes = [sds(owners // 2, rows, width), sds(owners // 4, rows, width), sds(owners // 4, rows, width)]
    else:
        shapes = [sds(owners, rows, width)]

    def kernel(*refs):
        gradient_kernel(rows, steps, relative, len(shapes), *refs)

    return pl.pallas_call(
        kernel,
        grid=(left.shape[1] // block, width // cols),
        in_specs=[
            pl.BlockSpec(memory_space=pltpu.SMEM),
            pl.BlockSpec((depth, block), lambda i, j: (0, i)),
            pl.BlockSpec((depth, cols), lambda i, j: (0, j + first // cols)),
        ],
        out_specs=[pl.BlockSpec(memory_space=pl.ANY)] * len(shapes),
        out_shape=shapes,
        scratch_shapes=[pltpu.VMEM((2, block, cols), BF), pltpu.SemaphoreType.DMA((2, block // rows))],
        compiler_params=pltpu.CompilerParams(vmem_limit_bytes=60 << 20),
        cost_estimate=cost(2.5 * depth * left.shape[1] * width, [left, right] + shapes),
        name=name,
    )(place, left, right)


SWAP = [(0, 1), (1, 0)]


def row(vector):
    return vector.reshape(1, -1).astype(F32)


def after(value, *others):
    return lax.optimization_barrier((value, others))[0]


def both_groups(shard):
    if lax.axis_size("dp") != 2:
        return lax.psum(shard, "dp").astype(F32)
    return shard.astype(F32) + lax.ppermute(shard, "dp", SWAP).astype(F32)


class Whole:
    def __init__(self, owners):
        self.owners, self.mine, self.relative = owners, jnp.zeros((2,), jnp.int32), False

    def gather_small(self, vector):
        return lax.all_gather(vector.reshape(1, -1), "fsdp", axis=0, tiled=True)

    def gather(self, w):
        return lax.all_gather(w, "fsdp", axis=0, tiled=True)

    def first_stage(self, parts, *before):
        return parts

    def second_stage(self, parts, *before):
        return parts

    def joined(self, parts):
        return (jnp.concatenate([p[0] for p in parts], 2),)

    def third_stage(self, parts):
        whole = parts[0].reshape(-1, parts[0].shape[2])
        return lax.psum_scatter(whole, "fsdp", scatter_dimension=0, tiled=True)

    def scatter_small(self, shares):
        return lax.psum(lax.psum_scatter(shares, "fsdp", scatter_dimension=0, tiled=True)[0], "dp")


class Split:
    relative = True

    def __init__(self, owners):
        self.owners, self.count = owners, owners // 4
        self.mine = jnp.stack([lax.axis_index("x"), lax.axis_index("core")]).astype(jnp.int32)
        self.z = jnp.arange(self.count, dtype=jnp.int32)

    def gather(self, w):
        return lax.all_gather(w, ("z", "x", "core"), axis=0, tiled=True)

    def gather_small(self, vector):
        rows = vector.reshape(1, -1)

        def double(rows, axis, step, other):
            got = lax.ppermute(rows, axis, other)
            low = lax.rem(lax.axis_index(axis) // step, 2) == 0
            return jnp.concatenate([jnp.where(low, rows, got), jnp.where(low, got, rows)], 0)
        rows = double(rows, "core", 1, SWAP)
        rows = double(rows, "x", 1, SWAP)
        step = 1
        while step < self.count:
            rows = double(rows, "z", step, [(i, i ^ step) for i in range(self.count)])
            step *= 2
        return rows

    def first_stage(self, parts, *before):
        send, keep, pass_on = parts
        half = send.shape[0] // 2
        got = lax.ppermute(send, "core", SWAP)
        return after(pass_on, *before) + got[half:], keep, got

    def second_stage(self, parts, *before):
        passed, keep, got = parts
        half, keep = got.shape[0] // 2, after(keep, *before)
        got_x = lax.ppermute(passed, "x", SWAP)
        return (keep.astype(F32) + got[:half].astype(F32) + got_x.astype(F32)).astype(BF)

    def joined(self, parts):
        return tuple(jnp.concatenate(a, 2) for a in zip(*parts))

    def third_stage(self, total):
        return lax.psum_scatter(total, "z", scatter_dimension=0, tiled=True)[0]

    def scatter_small(self, shares):
        shares = shares.reshape(self.count, 2, 2, -1)

        def halve(rows, axis, here):
            kept = lax.dynamic_index_in_dim(rows, here, axis, keepdims=False)
            return kept, lax.dynamic_index_in_dim(rows, 1 - here, axis, keepdims=False)
        kept, sent = halve(shares, 2, self.mine[1])
        shares = kept + lax.ppermute(sent, "core", SWAP)
        kept, sent = halve(shares, 1, self.mine[0])
        shares = kept + lax.ppermute(sent, "x", SWAP)
        step = self.count // 2
        while step:
            shares = shares.reshape(2, step, -1)
            kept, sent = halve(shares, 0, lax.rem(lax.axis_index("z") // step, 2))
            shares = kept + lax.ppermute(sent, "z", [(i, i ^ step) for i in range(self.count)])
            step //= 2
        shares = shares.reshape(-1)
        if lax.axis_size("dp") != 2:
            return lax.psum(shares, "dp")
        return shares + lax.ppermute(shares, "dp", SWAP)


def row(vector):
    return vector.reshape(1, -1).astype(F32)


def layer(links, images, cotangent, w_qkv, w_out, w_up, w_down, *vectors):
    n, owners = images.shape[0], links.owners

    sizes = [v.shape[0] for v in vectors]
    small = links.gather_small(jnp.concatenate(vectors))
    full, first = [], 0
    for size in sizes:
        full.append(row(small[:, first:first + size]))
        first += size
    b_qv, b_out, b_up, b_down, gain_one, shift_one, gain_two, shift_two = full

    def image(a):
        return (a, "image")

    def rows(*shape, dtype=BF):
        return (sds(n, *shape, dtype=dtype), "image")

    def sums(width):
        return total(sds(8, width, dtype=F32))

    def gradient(left, right, name, first=0, width=None):
        return weight_gradient(left, right, owners, links.mine, links.relative, name, first, width)

    def by_columns(kernel, weight, rows_in, others, outs, name, flops, sum_width=0):
        def cut(a):
            if len(a.shape) == 2:
                return a, pl.BlockSpec((a.shape[0], D), lambda j, i: (0, j))
            return a, pl.BlockSpec((4, SP, D), lambda j, i: (i, 0, j))
        results = [cut(a) for a in outs]
        return grid_call(
            kernel, (outs[0].shape[2] // D, n // 4),
            [weight, (rows_in, pl.BlockSpec((4, SP, D), lambda j, i: (i, 0, 0)))] + [cut(a) for a in others],
            results, name, flops * n * SP)

    full_qkv = links.gather(w_qkv)
    normed_one, xpad, cpad, s_down = call(
        prepare_kernel, n, [image(images), image(cotangent), whole(gain_one), whole(shift_one)],
        [rows(SP, D), rows(SP, D), rows(SP, D), sums(D)], "prepare", 8 * n * SP * D * 50)
    middle = links.gather(after(jnp.concatenate([w_up, w_out], 1), normed_one))
    full_out = middle, pl.BlockSpec((D, D), lambda *at: (0, FF // D), pipeline_mode=pl.Buffered(1))
    bias = jnp.concatenate([b_qv[:, :D], jnp.zeros((1, D), F32), b_qv[:, D:]], 1)
    packed, = by_columns(
        qkv_kernel, (full_qkv, pl.BlockSpec((D, D), lambda j, i: (0, j))), normed_one, [bias], [sds(n, SP, 3 * D)],
        "qkv", 2.5 * D * 3 * D)
    full_down = links.gather(after(w_down, packed))
    mixed, logsum = call(
        attention_kernel, n, [image(packed)], [rows(SP, D), rows(H, SP, dtype=F32)], "attention", 1e5 * n * SP * H)
    hidden, normed_two = call(
        out_kernel, n,
        [full_out, image(xpad), image(mixed), whole(b_out), whole(gain_two), whole(shift_two)],
        [rows(SP, D, dtype=F32), rows(SP, D)], "out", 3 * D * D * n * SP)
    active, slope = by_columns(
        up_kernel, (middle, pl.BlockSpec((D, D), lambda j, i: (0, j))), normed_two, [b_up], [sds(n, SP, FF)] * 2,
        "up", 4 * D * FF)

    p_down = gradient(active, cpad, "g_down")
    d_inner, s_up = by_columns(
        down_back_kernel, (full_down, pl.BlockSpec((D, D), lambda j, i: (j, 0))), after(cpad, p_down), [slope],
        [sds(n, SP, FF), sds(8, FF, dtype=F32)], "down_back", 3 * D * FF)
    p_down = links.first_stage(p_down, d_inner)
    p_up = gradient(normed_two, after(d_inner, p_down[0]), "g_up_low", 0, FF // 2)
    p_up2 = gradient(normed_two, after(d_inner, p_up), "g_up_high", FF // 2, FF // 2)
    p_up = links.first_stage(p_up, p_up2)

    def pair(a):
        return a, pl.BlockSpec((2,) + tuple(a.shape[1:]), lambda i, k: (i, 0, 0))
    d_hidden, d_hidden_b, d_mixed, s_gain_two, s_shift_two, s_out = grid_call(
        up_back_kernel, (n // 2, 2),
        [(middle, pl.BlockSpec((D, FF // 2), lambda i, k: (0, k))),
         (after(d_inner, p_up2, p_up[0]), pl.BlockSpec((2, SP, FF // 2), lambda i, k: (i, 0, k))),
         full_out, pair(hidden), pair(cpad), whole(gain_two)],
        [pair(sds(n, SP, D, dtype=F32)), pair(sds(n, SP, D)), pair(sds(n, SP, D)), sums(D), sums(D), sums(D)],
        "up_back", 3 * D * (D + FF) * n * SP, [pltpu.VMEM((2 * SP, D), F32)])
    p_down = links.second_stage(p_down, d_hidden_b)
    p_up = links.second_stage(p_up, d_hidden_b)
    p_out = gradient(mixed, after(d_hidden_b, p_down, p_up), "g_out")
    p_down = links.third_stage(p_down)
    p_up2 = links.first_stage(p_up2, p_out)
    p_out = links.first_stage(p_out)
    rest = links.joined([p_up2, p_out])
    d_packed, s_qv = call(
        attention_back_kernel, n, [image(packed), image(mixed), image(after(d_mixed, rest[0])), image(logsum)],
        [rows(SP, 3 * D), sums(2 * D)], "attention_back", 1.4e5 * n * SP * H)
    rest = links.second_stage(rest, d_packed)
    p_up = links.third_stage(after(p_up, p_down, d_packed))
    last = gradient(normed_one, after(d_packed, rest, p_down), "g_qkv")
    last = links.first_stage(after(last, p_up))
    rest = links.third_stage(after(rest, p_up))
    staging = [pltpu.VMEM((D // 128, SEQ * n, 128), F32), pltpu.SemaphoreType.DMA((D // 128,))]
    d_images, s_gain_one, s_shift_one = call(
        qkv_back_kernel, n,
        [whole(full_qkv), image(after(d_packed, last[0])), image(xpad), image(d_hidden), whole(gain_one)],
        [untouched(sds(SEQ * n, D, dtype=F32)), sums(D), sums(D)], "qkv_back", 3 * D * 3 * D * n * SP, staging)
    g_down, g_up = both_groups(after(p_down, last[0])), both_groups(after(p_up, last[0]))
    last = links.second_stage(last, d_images, rest, g_down, g_up)
    result, = call(
        down_kernel, n, [whole(full_down), image(after(active, last)), image(hidden), whole(b_down)],
        [untouched(sds(SEQ * n, D, dtype=F32))], "down", 2.5 * D * FF * n * SP, staging)
    rest = both_groups(after(rest, last))
    last, rest, s_gain_one = after((links.third_stage(last), rest, s_gain_one), result)
    g_qkv = both_groups(last)
    g_up2, g_out = rest[:, :FF // 2], rest[:, FF // 2:]
    result, d_images = [jnp.transpose(a.reshape(SEQ, n, D), (1, 0, 2)) for a in (result, d_images)]
    g_up = jnp.concatenate([g_up, g_up2], 1)

    parts = [s_qv, s_out, s_up, s_down, s_gain_one, s_shift_one, s_gain_two, s_shift_two]
    share = links.scatter_small(jnp.concatenate([jnp.sum(s, 0).reshape(owners, -1) for s in parts], 1))
    small_grads, first = [], 0
    for size in sizes:
        small_grads.append(share[first:first + size])
        first += size
    return (result, d_images, g_qkv, g_out, g_up, g_down, *small_grads)


def solution(mesh):
    dp, owners = mesh.shape["dp"], mesh.shape["fsdp"]
    kind, fsdp = Whole, ("fsdp",)
    if dp == 2 and owners % 4 == 0 and (D // owners) % 16 == 0:
        kind, fsdp = Split, ("z", "x", "core")
        mesh = Mesh(mesh.devices.reshape(dp, owners // 4, 2, 2), ("dp",) + fsdp)
    images, matrix, vector = P(("dp",) + fsdp, None, None), P(fsdp, None), P(fsdp)
    specs = (images,) * 2 + (matrix,) * 4 + (vector,) * 8

    def run(*args):
        return layer(kind(owners), *args)

    return jax.shard_map(run, mesh=mesh, in_specs=specs, out_specs=specs, check_vma=False)
```

```python
import math

import jax
import jax.numpy as jnp
from jax import lax
from jax.experimental import pallas as pl
from jax.experimental.pallas import tpu as pltpu
from jax.sharding import Mesh
from jax.sharding import PartitionSpec as P

D = 1280
H = 16
HD = 80
FF = 5120
SEQ = 257
SP = 264
GROUP = 8
GW = GROUP * HD
EPS = 1e-06
SCALE = HD ** (-0.5)
NT = (((1,), (1,)), ((), ()))
BF = jnp.bfloat16
F32 = jnp.float32


def dot_nt(left, right):
    return lax.dot_general(left, right, NT, preferred_element_type=F32)


def dot_nn(left, right):
    return jnp.dot(left, right, preferred_element_type=F32)


def pad_rows(rows):
    return jnp.concatenate([rows, jnp.zeros((SP - SEQ, rows.shape[1]), rows.dtype)], 0)


def fold_rows(rows):
    return jnp.sum(rows.reshape(rows.shape[0] // 8, 8, rows.shape[1]), 0)


def standardize(rows):
    centered = rows - jnp.mean(rows, -1, keepdims=True)
    inverse = lax.rsqrt(jnp.mean(centered * centered, -1, keepdims=True) + EPS)
    return centered * inverse, inverse


def norm_gradient(e, xhat, inverse, gain):
    scaled = e * gain
    first = jnp.mean(scaled, -1, keepdims=True)
    second = jnp.mean(scaled * xhat, -1, keepdims=True)
    return inverse * (scaled - first - xhat * second)


def cost(flops, arrays):
    moved = sum(math.prod(a.shape) * a.dtype.itemsize for a in arrays)
    return pl.CostEstimate(flops=int(flops), transcendentals=0, bytes_accessed=moved)


def grid_call(kernel, grid, ins, outs, name, flops=0, scratch=()):
    return pl.pallas_call(
        kernel,
        grid=grid,
        in_specs=[spec for _, spec in ins],
        out_specs=[spec for _, spec in outs],
        out_shape=[a for a, _ in outs],
        scratch_shapes=list(scratch),
        compiler_params=pltpu.CompilerParams(vmem_limit_bytes=62 << 20),
        cost_estimate=cost(flops, [a for a, _ in ins] + [a for a, _ in outs]),
        name=name,
    )(*[a for a, _ in ins])


def whole(a):
    return a, pl.BlockSpec(tuple(a.shape), lambda *at: (0,) * len(a.shape), pipeline_mode=pl.Buffered(1))


def total(a):
    return a, pl.BlockSpec(tuple(a.shape), lambda *at: (0,) * len(a.shape))


def untouched(a):
    return a, pl.BlockSpec(memory_space=pl.ANY)


def call(kernel, n, ins, outs, name, flops=0, scratch=()):
    def specs(pairs):
        for a, kind in pairs:
            if kind == "image":
                kind = pl.BlockSpec((1,) + tuple(a.shape[1:]), lambda i, last=len(a.shape) - 1: (i,) + (0,) * last)
            yield a, kind
    return grid_call(kernel, (n,), list(specs(ins)), list(specs(outs)), name, flops, scratch)


def accumulate(ref, value):
    @pl.when(pl.program_id(0) == 0)
    def _():
        ref[...] = jnp.zeros_like(ref)
    ref[...] += value


def prepare_kernel(x_ref, c_ref, gain_ref, shift_ref, normed_ref, xpad_ref, cpad_ref, sum_ref):
    x = x_ref[0].astype(F32)
    xhat, _ = standardize(x)
    normed = xhat * gain_ref[...] + shift_ref[...]
    normed_ref[0] = pad_rows(normed).astype(BF)
    xpad_ref[0] = pad_rows(x).astype(BF)
    c = pad_rows(c_ref[0].astype(F32))
    cpad_ref[0] = c.astype(BF)
    accumulate(sum_ref, fold_rows(c))


def flat(ref):
    return ref[...].reshape(ref.shape[0] * ref.shape[1], ref.shape[2])


def qkv_kernel(w_ref, normed_ref, bias_ref, packed_ref):
    out = dot_nn(flat(normed_ref), w_ref[...]) + bias_ref[...]
    packed_ref[...] = out.astype(BF).reshape(packed_ref.shape)


def drop_tail(rows):
    tail = rows[SP - 8:]
    keep = lax.broadcasted_iota(jnp.int32, tail.shape, 0) < SEQ - (SP - 8)
    return jnp.concatenate([rows[:SP - 8], jnp.where(keep, tail, 0.0)], 0)


def attention_kernel(packed_ref, mixed_ref, lse_ref):
    def group(g, carry):
        base = g * GW
        here = pl.ds(pl.multiple_of(base, 128), GW)
        queries, keys, values = [
            packed_ref[0, :, pl.ds(pl.multiple_of(part * D + base, 128), GW)] for part in range(3)]
        values_t = values.astype(F32).T.astype(BF)
        outs, lses = [], []
        for j in range(GROUP):
            head = slice(j * HD, (j + 1) * HD)
            s = dot_nt(keys[:, head], queries[:, head])
            tail = s[SP - 8:]
            keep = lax.broadcasted_iota(jnp.int32, tail.shape, 0) < SEQ - (SP - 8)
            s = jnp.concatenate([s[:SP - 8], jnp.where(keep, tail, -1e30)], 0) * SCALE
            top = jnp.max(s, 0, keepdims=True)
            e = jnp.exp(s - top)
            total = jnp.sum(e, 0, keepdims=True)
            o = dot_nn(values_t[head], e.astype(BF)) * (1.0 / total)
            outs.append(o)
            lses.append(top + jnp.log(total))
        mixed_ref[0, :, pl.ds(pl.multiple_of(base, 128), GW)] = jnp.concatenate(outs, 0).T.astype(BF)
        lse_ref[0, pl.ds(pl.multiple_of(g * GROUP, 8), GROUP), :] = jnp.concatenate(lses, 0)
        return carry
    lax.fori_loop(0, H // GROUP, group, 0)


def out_kernel(w_ref, x_ref, mixed_ref, bias_ref, gain_ref, shift_ref, hidden_ref, normed_ref):
    hidden = flat(x_ref).astype(F32) + dot_nn(flat(mixed_ref), w_ref[...]) + bias_ref[...]
    hidden_ref[...] = hidden.reshape(hidden_ref.shape)
    xhat, _ = standardize(hidden)
    normed = xhat * gain_ref[...] + shift_ref[...]
    keep = lax.rem(lax.broadcasted_iota(jnp.int32, normed.shape, 0), SP) < SEQ
    normed_ref[...] = jnp.where(keep, normed, 0.0).astype(BF).reshape(normed_ref.shape)


def up_kernel(w_ref, normed_ref, bias_ref, active_ref, slope_ref):
    u = dot_nn(flat(normed_ref), w_ref[...]) + bias_ref[...]
    cdf = 0.5 * (1.0 + lax.erf(u * 0.7071067811865476))
    active_ref[...] = (u * cdf).astype(BF).reshape(active_ref.shape)
    slope_ref[...] = (cdf + u * jnp.exp(-0.5 * u * u) * 0.3989422804014327).astype(BF).reshape(slope_ref.shape)


def interleave(rows, out_ref, stage_ref, sems):
    image, last = pl.program_id(0), pl.num_programs(0) - 1
    tiles = stage_ref.shape[0]
    step = stage_ref.shape[1] // SEQ
    for k in range(tiles):
        stage_ref[k, pl.ds(image, SEQ, stride=step), :] = rows[:SEQ, k * 128:(k + 1) * 128]

    @pl.when(image == last)
    def _():
        copies = [pltpu.make_async_copy(stage_ref.at[k], out_ref.at[:, k * 128:(k + 1) * 128], sems.at[k]) for k in range(tiles)]
        for copy in copies:
            copy.start()
        for copy in copies:
            copy.wait()


def down_kernel(w_ref, active_ref, hidden_ref, bias_ref, result_ref, stage_ref, sems):
    result = hidden_ref[0] + dot_nn(active_ref[0], w_ref[...]) + bias_ref[...]
    interleave(result, result_ref, stage_ref, sems)


def down_back_kernel(w_ref, c_ref, slope_ref, dinner_ref, sum_ref):
    d = dot_nt(flat(c_ref), w_ref[...]) * flat(slope_ref).astype(F32)
    dinner_ref[...] = d.astype(BF).reshape(dinner_ref.shape)

    @pl.when(pl.program_id(1) == 0)
    def _():
        sum_ref[...] = jnp.zeros_like(sum_ref)
    sum_ref[...] += fold_rows(d)


def up_back_kernel(w_up_ref, dinner_ref, w_out_ref, hidden_ref, c_ref, gain_ref,
                   dhidden_ref, dhidden_b_ref, dmixed_ref, sum_gain_ref, sum_shift_ref, sum_out_ref, acc_ref):
    i, k = pl.program_id(0), pl.program_id(1)

    @pl.when(k == 0)
    def _():
        acc_ref[...] = dot_nt(flat(dinner_ref), w_up_ref[...])

    @pl.when(k > 0)
    def _():
        acc_ref[...] += dot_nt(flat(dinner_ref), w_up_ref[...])

    @pl.when(jnp.logical_and(i == 0, k == 0))
    def _():
        for ref in (sum_gain_ref, sum_shift_ref, sum_out_ref):
            ref[...] = jnp.zeros_like(ref)

    @pl.when(k == pl.num_programs(1) - 1)
    def _():
        for image in range(dhidden_ref.shape[0]):
            e = acc_ref[image * SP:(image + 1) * SP]
            xhat, inverse = standardize(hidden_ref[image])
            dhidden = c_ref[image].astype(F32) + norm_gradient(e, xhat, inverse, gain_ref[...])
            dhidden_ref[image] = dhidden
            dhidden_b = dhidden.astype(BF)
            dhidden_b_ref[image] = dhidden_b
            dmixed_ref[image] = dot_nt(dhidden_b, w_out_ref[...]).astype(BF)
            sum_gain_ref[...] += fold_rows(e * xhat)
            sum_shift_ref[...] += fold_rows(e)
            sum_out_ref[...] += fold_rows(dhidden)


def attention_back_kernel(packed_ref, mixed_ref, dmixed_ref, lse_ref, dpacked_ref, sum_ref):
    full = SEQ - 1

    @pl.when(pl.program_id(0) == 0)
    def _():
        sum_ref[...] = jnp.zeros_like(sum_ref)

    def group(g, carry):
        base = g * GW
        queries, keys, values = [
            packed_ref[0, :, pl.ds(pl.multiple_of(part * D + base, 128), GW)] for part in range(3)]
        here = pl.ds(pl.multiple_of(base, 128), GW)
        grads = dmixed_ref[0, :, here]
        product = grads.astype(F32) * mixed_ref[0, :, here].astype(F32)
        product_t = product[:full].T
        keys_t = keys.astype(F32).T
        keys_tb = keys_t[:, :full].astype(BF)
        lse = lse_ref[0, pl.ds(pl.multiple_of(g * GROUP, 8), GROUP), :]
        dq, dk, dv = [], [], []
        for j in range(GROUP):
            head = slice(j * HD, (j + 1) * HD)
            q, k, v, dm = queries[:full, head], keys[:, head], values[:, head], grads[:full, head]
            delta = jnp.sum(product_t[head], 0, keepdims=True)
            p = drop_tail(jnp.exp(dot_nt(k, q) * SCALE - lse[j:j + 1, :full]))
            dv.append(dot_nn(p.astype(BF), dm))
            ds = (p * (dot_nt(v, dm) - delta) * SCALE).astype(BF)
            dk.append(dot_nn(ds, q))
            dq.append(dot_nn(keys_tb[head], ds[:full])
                      + keys_t[head, full:full + 1] * ds[full:].astype(F32)[:1])
        dq = jnp.concatenate(dq, 0).T
        dk = jnp.concatenate(dk, 1)
        dv = jnp.concatenate(dv, 1)

        head_row = lax.broadcasted_iota(jnp.int32, (GROUP, GW), 0)
        lane = lax.broadcasted_iota(jnp.int32, (GROUP, GW), 1)
        mine = jnp.logical_and(lane >= head_row * HD, lane < (head_row + 1) * HD)
        diagonal = lax.broadcasted_iota(jnp.int32, (GROUP, GROUP), 0) == lax.broadcasted_iota(jnp.int32, (GROUP, GROUP), 1)

        def spread(rows):
            return jnp.where(mine, rows[full:].astype(F32)[:1], 0.0)

        def as_row(column):
            return jnp.sum(jnp.where(diagonal, column, 0.0), 0, keepdims=True)
        q, dm = spread(queries).astype(BF), spread(grads).astype(BF)
        delta = as_row(jnp.sum(spread(product), 1, keepdims=True))
        p = drop_tail(jnp.exp(dot_nt(keys, q) * SCALE - as_row(lse[:, full:full + 1])))
        ds = p * (dot_nt(values, dm) - delta) * SCALE
        dv = dv + dot_nn(p.astype(BF), dm)
        dk = dk + dot_nn(ds.astype(BF), q)
        ds_t = jnp.concatenate([ds, jnp.zeros((SP, 128 - GROUP), F32)], 1).T[:GROUP].astype(BF)
        dq_last = jnp.sum(jnp.where(mine, dot_nn(ds_t, keys), 0.0), 0, keepdims=True)
        tail = lax.broadcasted_iota(jnp.int32, (SP - full, GW), 0) == 0
        dq_last = jnp.where(tail, dq_last, 0.0)

        def out(part):
            return pl.ds(pl.multiple_of(part * D + base, 128), GW)
        dpacked_ref[0, :full, out(0)] = dq.astype(BF)
        dpacked_ref[0, full:, out(0)] = dq_last.astype(BF)
        dpacked_ref[0, :, out(1)] = dk.astype(BF)
        dpacked_ref[0, :, out(2)] = dv.astype(BF)
        sum_ref[:, out(0)] += fold_rows(dq) + dq_last
        sum_ref[:, out(1)] += fold_rows(dv)
        return carry
    lax.fori_loop(0, H // GROUP, group, 0)


def qkv_back_kernel(w_ref, dpacked_ref, x_ref, dhidden_ref, gain_ref,
                    dimages_ref, sum_gain_ref, sum_shift_ref, stage_ref, sems):
    e = dot_nt(dpacked_ref[0], w_ref[...])
    xhat, inverse = standardize(x_ref[0].astype(F32))
    dimages = dhidden_ref[0] + norm_gradient(e, xhat, inverse, gain_ref[...])
    interleave(dimages, dimages_ref, stage_ref, sems)
    accumulate(sum_gain_ref, fold_rows(e * xhat))
    accumulate(sum_shift_ref, fold_rows(e))


def sds(*shape, dtype=BF):
    return jax.ShapeDtypeStruct(shape, dtype)


def gradient_kernel(rows, steps, relative, spots, place_ref, l_ref, r_ref, *rest):
    outs, stage, sems = rest[:spots], rest[spots], rest[spots + 1]
    i, j = pl.program_id(0), pl.program_id(1)
    step = i * pl.num_programs(1) + j
    block, width = stage.shape[1], stage.shape[2]
    per = block // rows

    def copy(slot, t, out, at, cols):
        return pltpu.make_async_copy(stage.at[slot, t * rows:(t + 1) * rows, :], out.at[at, :, cols], sems.at[slot, t])

    def drain(slot):
        for t in range(per):
            copy(slot, t, outs[0], 0, pl.ds(0, width)).wait()

    slot = lax.rem(step, 2)

    @pl.when(step >= 2)
    def _():
        drain(slot)
    stage[slot] = lax.dot_general(l_ref[...], r_ref[...], (((0,), (0,)), ((), ())), preferred_element_type=F32).astype(BF)
    cols = pl.ds(pl.multiple_of(j * width, 128), width)
    for t in range(per):
        owner = i * per + t
        if not relative:
            copy(slot, t, outs[0], owner, cols).start()
            continue
        core = lax.rem(owner, 2) ^ place_ref[1]
        x = lax.rem(owner // 2, 2) ^ place_ref[0]
        z = owner // 4

        @pl.when(core == 1)
        def _():
            copy(slot, t, outs[0], x * (outs[0].shape[0] // 2) + z, cols).start()

        @pl.when(jnp.logical_and(core == 0, x == 0))
        def _():
            copy(slot, t, outs[1], z, cols).start()

        @pl.when(jnp.logical_and(core == 0, x == 1))
        def _():
            copy(slot, t, outs[2], z, cols).start()

    @pl.when(step == steps - 1)
    def _():
        drain(slot)
        if steps > 1:
            drain(1 - slot)


def weight_gradient(left, right, owners, place, relative, name, first=0, width=None):
    depth = left.shape[0] * left.shape[1]
    left, right = left.reshape(depth, -1), right.reshape(depth, -1)
    block, cols, width = 640, 640, width or right.shape[1]
    if not relative:
        owners = left.shape[1] // block
    rows = left.shape[1] // owners
    steps = (left.shape[1] // block) * (width // cols)
    if relative:
        shapes = [sds(owners // 2, rows, width), sds(owners // 4, rows, width), sds(owners // 4, rows, width)]
    else:
        shapes = [sds(owners, rows, width)]

    def kernel(*refs):
        gradient_kernel(rows, steps, relative, len(shapes), *refs)

    return pl.pallas_call(
        kernel,
        grid=(left.shape[1] // block, width // cols),
        in_specs=[
            pl.BlockSpec(memory_space=pltpu.SMEM),
            pl.BlockSpec((depth, block), lambda i, j: (0, i)),
            pl.BlockSpec((depth, cols), lambda i, j: (0, j + first // cols)),
        ],
        out_specs=[pl.BlockSpec(memory_space=pl.ANY)] * len(shapes),
        out_shape=shapes,
        scratch_shapes=[pltpu.VMEM((2, block, cols), BF), pltpu.SemaphoreType.DMA((2, block // rows))],
        compiler_params=pltpu.CompilerParams(vmem_limit_bytes=60 << 20),
        cost_estimate=cost(2.5 * depth * left.shape[1] * width, [left, right] + shapes),
        name=name,
    )(place, left, right)


SWAP = [(0, 1), (1, 0)]


def row(vector):
    return vector.reshape(1, -1).astype(F32)


def after(value, *others):
    return lax.optimization_barrier((value, others))[0]


def both_groups(shard):
    if lax.axis_size("dp") != 2:
        return lax.psum(shard, "dp").astype(F32)
    return shard.astype(F32) + lax.ppermute(shard, "dp", SWAP).astype(F32)


class Whole:
    def __init__(self, owners):
        self.owners, self.mine, self.relative = owners, jnp.zeros((2,), jnp.int32), False

    def gather_small(self, vector):
        return lax.all_gather(vector.reshape(1, -1), "fsdp", axis=0, tiled=True)

    def gather(self, w):
        return lax.all_gather(w, "fsdp", axis=0, tiled=True)

    def first_stage(self, parts, *before):
        return parts

    def second_stage(self, parts, *before):
        return parts

    def joined(self, parts):
        return (jnp.concatenate([p[0] for p in parts], 2),)

    def third_stage(self, parts):
        whole = parts[0].reshape(-1, parts[0].shape[2])
        return lax.psum_scatter(whole, "fsdp", scatter_dimension=0, tiled=True)

    def scatter_small(self, shares):
        return lax.psum(lax.psum_scatter(shares, "fsdp", scatter_dimension=0, tiled=True)[0], "dp")


class Split:
    relative = True

    def __init__(self, owners):
        self.owners, self.count = owners, owners // 4
        self.mine = jnp.stack([lax.axis_index("x"), lax.axis_index("core")]).astype(jnp.int32)
        self.z = jnp.arange(self.count, dtype=jnp.int32)

    def gather(self, w):
        return lax.all_gather(w, ("z", "x", "core"), axis=0, tiled=True)

    def gather_small(self, vector):
        rows = vector.reshape(1, -1)

        def double(rows, axis, step, other):
            got = lax.ppermute(rows, axis, other)
            low = lax.rem(lax.axis_index(axis) // step, 2) == 0
            return jnp.concatenate([jnp.where(low, rows, got), jnp.where(low, got, rows)], 0)
        rows = double(rows, "core", 1, SWAP)
        rows = double(rows, "x", 1, SWAP)
        step = 1
        while step < self.count:
            rows = double(rows, "z", step, [(i, i ^ step) for i in range(self.count)])
            step *= 2
        return rows

    def first_stage(self, parts, *before):
        send, keep, pass_on = parts
        half = send.shape[0] // 2
        got = lax.ppermute(send, "core", SWAP)
        return after(pass_on, *before) + got[half:], keep, got

    def second_stage(self, parts, *before):
        passed, keep, got = parts
        half, keep = got.shape[0] // 2, after(keep, *before)
        got_x = lax.ppermute(passed, "x", SWAP)
        return (keep.astype(F32) + got[:half].astype(F32) + got_x.astype(F32)).astype(BF)

    def joined(self, parts):
        return tuple(jnp.concatenate(a, 2) for a in zip(*parts))

    def third_stage(self, total):
        return lax.psum_scatter(total, "z", scatter_dimension=0, tiled=True)[0]

    def scatter_small(self, shares):
        shares = shares.reshape(self.count, 2, 2, -1)

        def halve(rows, axis, here):
            kept = lax.dynamic_index_in_dim(rows, here, axis, keepdims=False)
            return kept, lax.dynamic_index_in_dim(rows, 1 - here, axis, keepdims=False)
        kept, sent = halve(shares, 2, self.mine[1])
        shares = kept + lax.ppermute(sent, "core", SWAP)
        kept, sent = halve(shares, 1, self.mine[0])
        shares = kept + lax.ppermute(sent, "x", SWAP)
        step = self.count // 2
        while step:
            shares = shares.reshape(2, step, -1)
            kept, sent = halve(shares, 0, lax.rem(lax.axis_index("z") // step, 2))
            shares = kept + lax.ppermute(sent, "z", [(i, i ^ step) for i in range(self.count)])
            step //= 2
        shares = shares.reshape(-1)
        if lax.axis_size("dp") != 2:
            return lax.psum(shares, "dp")
        return shares + lax.ppermute(shares, "dp", SWAP)


def row(vector):
    return vector.reshape(1, -1).astype(F32)


def layer(links, images, cotangent, w_qkv, w_out, w_up, w_down, *vectors):
    n, owners = images.shape[0], links.owners

    sizes = [v.shape[0] for v in vectors]
    small = links.gather_small(jnp.concatenate(vectors))
    full, first = [], 0
    for size in sizes:
        full.append(row(small[:, first:first + size]))
        first += size
    b_qv, b_out, b_up, b_down, gain_one, shift_one, gain_two, shift_two = full

    def image(a):
        return (a, "image")

    def rows(*shape, dtype=BF):
        return (sds(n, *shape, dtype=dtype), "image")

    def sums(width):
        return total(sds(8, width, dtype=F32))

    def gradient(left, right, name, first=0, width=None):
        return weight_gradient(left, right, owners, links.mine, links.relative, name, first, width)

    def by_columns(kernel, weight, rows_in, others, outs, name, flops, sum_width=0):
        def cut(a):
            if len(a.shape) == 2:
                return a, pl.BlockSpec((a.shape[0], D), lambda j, i: (0, j))
            return a, pl.BlockSpec((4, SP, D), lambda j, i: (i, 0, j))
        results = [cut(a) for a in outs]
        return grid_call(
            kernel, (outs[0].shape[2] // D, n // 4),
            [weight, (rows_in, pl.BlockSpec((4, SP, D), lambda j, i: (i, 0, 0)))] + [cut(a) for a in others],
            results, name, flops * n * SP)

    full_qkv = links.gather(w_qkv)
    normed_one, xpad, cpad, s_down = call(
        prepare_kernel, n, [image(images), image(cotangent), whole(gain_one), whole(shift_one)],
        [rows(SP, D), rows(SP, D), rows(SP, D), sums(D)], "prepare", 8 * n * SP * D * 50)
    middle = links.gather(after(jnp.concatenate([w_up, w_out], 1), normed_one))
    full_out = middle, pl.BlockSpec((D, D), lambda *at: (0, FF // D), pipeline_mode=pl.Buffered(1))
    bias = jnp.concatenate([b_qv[:, :D], jnp.zeros((1, D), F32), b_qv[:, D:]], 1)
    packed, = by_columns(
        qkv_kernel, (full_qkv, pl.BlockSpec((D, D), lambda j, i: (0, j))), normed_one, [bias], [sds(n, SP, 3 * D)],
        "qkv", 2.5 * D * 3 * D)
    full_down = links.gather(after(w_down, packed))
    mixed, logsum = call(
        attention_kernel, n, [image(packed)], [rows(SP, D), rows(H, SP, dtype=F32)], "attention", 1e5 * n * SP * H)
    hidden, normed_two = call(
        out_kernel, n,
        [full_out, image(xpad), image(mixed), whole(b_out), whole(gain_two), whole(shift_two)],
        [rows(SP, D, dtype=F32), rows(SP, D)], "out", 3 * D * D * n * SP)
    active, slope = by_columns(
        up_kernel, (middle, pl.BlockSpec((D, D), lambda j, i: (0, j))), normed_two, [b_up], [sds(n, SP, FF)] * 2,
        "up", 4 * D * FF)

    p_down = gradient(active, cpad, "g_down")
    d_inner, s_up = by_columns(
        down_back_kernel, (full_down, pl.BlockSpec((D, D), lambda j, i: (j, 0))), after(cpad, p_down), [slope],
        [sds(n, SP, FF), sds(8, FF, dtype=F32)], "down_back", 3 * D * FF)
    p_down = links.first_stage(p_down, d_inner)
    p_up = gradient(normed_two, after(d_inner, p_down[0]), "g_up_low", 0, FF // 2)
    p_up2 = gradient(normed_two, after(d_inner, p_up), "g_up_high", FF // 2, FF // 2)
    p_up = links.first_stage(p_up, p_up2)

    def pair(a):
        return a, pl.BlockSpec((2,) + tuple(a.shape[1:]), lambda i, k: (i, 0, 0))
    d_hidden, d_hidden_b, d_mixed, s_gain_two, s_shift_two, s_out = grid_call(
        up_back_kernel, (n // 2, 2),
        [(middle, pl.BlockSpec((D, FF // 2), lambda i, k: (0, k))),
         (after(d_inner, p_up2, p_up[0]), pl.BlockSpec((2, SP, FF // 2), lambda i, k: (i, 0, k))),
         full_out, pair(hidden), pair(cpad), whole(gain_two)],
        [pair(sds(n, SP, D, dtype=F32)), pair(sds(n, SP, D)), pair(sds(n, SP, D)), sums(D), sums(D), sums(D)],
        "up_back", 3 * D * (D + FF) * n * SP, [pltpu.VMEM((2 * SP, D), F32)])
    p_down = links.second_stage(p_down, d_hidden_b)
    p_up = links.second_stage(p_up, d_hidden_b)
    p_out = gradient(mixed, after(d_hidden_b, p_down, p_up), "g_out")
    p_down = links.third_stage(p_down)
    p_up2 = links.first_stage(p_up2, p_out)
    p_out = links.first_stage(p_out)
    rest = links.joined([p_up2, p_out])
    d_packed, s_qv = call(
        attention_back_kernel, n, [image(packed), image(mixed), image(after(d_mixed, rest[0])), image(logsum)],
        [rows(SP, 3 * D), sums(2 * D)], "attention_back", 1.4e5 * n * SP * H)
    rest = links.second_stage(rest, d_packed)
    p_up = links.third_stage(after(p_up, p_down, d_packed))
    last = gradient(normed_one, after(d_packed, rest, p_down), "g_qkv")
    last = links.first_stage(after(last, p_up))
    rest = links.third_stage(after(rest, p_up))
    staging = [pltpu.VMEM((D // 128, SEQ * n, 128), F32), pltpu.SemaphoreType.DMA((D // 128,))]
    d_images, s_gain_one, s_shift_one = call(
        qkv_back_kernel, n,
        [whole(full_qkv), image(after(d_packed, last[0])), image(xpad), image(d_hidden), whole(gain_one)],
        [untouched(sds(SEQ * n, D, dtype=F32)), sums(D), sums(D)], "qkv_back", 3 * D * 3 * D * n * SP, staging)
    g_down, g_up = both_groups(after(p_down, last[0])), both_groups(after(p_up, last[0]))
    last = links.second_stage(last, d_images, rest, g_down, g_up)
    result, = call(
        down_kernel, n, [whole(full_down), image(after(active, last)), image(hidden), whole(b_down)],
        [untouched(sds(SEQ * n, D, dtype=F32))], "down", 2.5 * D * FF * n * SP, staging)
    rest = both_groups(after(rest, last))
    last, rest, s_gain_one = after((links.third_stage(last), rest, s_gain_one), result)
    g_qkv = both_groups(last)
    g_up2, g_out = rest[:, :FF // 2], rest[:, FF // 2:]
    result, d_images = [jnp.transpose(a.reshape(SEQ, n, D), (1, 0, 2)) for a in (result, d_images)]
    g_up = jnp.concatenate([g_up, g_up2], 1)

    parts = [s_qv, s_out, s_up, s_down, s_gain_one, s_shift_one, s_gain_two, s_shift_two]
    share = links.scatter_small(jnp.concatenate([jnp.sum(s, 0).reshape(owners, -1) for s in parts], 1))
    small_grads, first = [], 0
    for size in sizes:
        small_grads.append(share[first:first + size])
        first += size
    return (result, d_images, g_qkv, g_out, g_up, g_down, *small_grads)


def solution(mesh):
    dp, owners = mesh.shape["dp"], mesh.shape["fsdp"]
    kind, fsdp = Whole, ("fsdp",)
    if dp == 2 and owners % 4 == 0 and (D // owners) % 16 == 0:
        kind, fsdp = Split, ("z", "x", "core")
        mesh = Mesh(mesh.devices.reshape(dp, owners // 4, 2, 2), ("dp",) + fsdp)
    images, matrix, vector = P(("dp",) + fsdp, None, None), P(fsdp, None), P(fsdp)
    specs = (images,) * 2 + (matrix,) * 4 + (vector,) * 8

    def run(*args):
        return layer(kind(owners), *args)

    return jax.shard_map(run, mesh=mesh, in_specs=specs, out_specs=specs, check_vma=False)
```
